32 devices in a mesh: groups: 2 (over y), tile: 16 (over z, x, core).
Axes of the slice: x: 2, y: 2, z: 4, core: 2. Of those that a mesh axis runs over, the one named last changes fastest.
Arguments:
- object_field: float32 [4, 2, 2048, 1024], P('groups', None, 'tile'), parts along dimension 0, may hold values from -7.6 to 7.6
- probe_modes: float32 [8, 2, 128, 128], P('groups'), parts along dimension 0, may hold values from -2.1 to 2.1
- measured: float32 [192, 128, 128], P(('groups', 'tile')), parts along dimension 0, may hold values from 0 to 2
- row_offset: int32 [192], P(('groups', 'tile')), parts along dimension 0, may hold values from 0 to 127, as said below
- col_offset: int32 [192], P(('groups', 'tile')), parts along dimension 0, may hold values from 0 to 896
- tile_counts: int32 [32], P('groups'), parts along dimension 0, may hold values from 1 to 6, as said below
Outputs:
- updated_object: float32 [4, 2, 2048, 1024], P('groups', None, 'tile'), parts along dimension 0
- updated_probe: float32 [8, 2, 128, 128], P('groups'), parts along dimension 0
The draws below stay inside these ranges and needn't reach their ends.
There are 2 independent parts, one for each index of `groups`. The reference program is written for one: setup_inputs(seed, part) draws one part's arguments, and reference() takes and returns one part's arrays. A program takes and returns all parts, laid end to end along the dimension named above; each array names one. Nothing has to cross between parts.
Inputs may be any that keep to these rules, and one draw needn't show every extreme that they name: `row_offset`: on the last tile a window's first row is at most 0, so windows never leave the object. The live positions of tile t fill its first tile_counts[t] slots; offsets and patterns of the other slots are unused.
All inputs are finite; a program needn't handle non-finite values.
Results may differ from the reference program's by a relative error of at most 0.0001.
Values sent between devices are 32-bit elements; how exact they have to be, the bound alone decides.
No kernel may reach another device: no remote copies, remote signals or barrier semaphores. Data moves between devices by JAX's collectives and lax.ppermute only.
A program may use at most 128 MiB of HBM per device.

```python
import math
import jax
import jax.numpy as jnp
from jax import lax

WIN = 128
MODES = 4
SLICES = 2
TX = 128
TY = 1024
P_MAX = 6
TILES = 16
ROWS = 2048
POSITIONS = 96


def draw_object_field(key, part):
    normal_key, column_key = jax.random.split(key, 2)
    row_frac = jnp.arange(ROWS).astype(jnp.float32) / ROWS
    column_frac = jax.random.uniform(column_key, (TY,), jnp.float32)
    scaling = 0.6 * jnp.power(10.0, 0.25 * row_frac)[:, None] * jnp.power(10.0, 0.25 * column_frac)[None, :]
    values = jnp.clip(jax.random.normal(normal_key, (SLICES, 2, ROWS, TY), jnp.float32), -4.0, 4.0)
    return (values * scaling).astype(jnp.float32)


def draw_row_offset(key, part):
    main_key, last_key = jax.random.split(key, 2)
    offsets = jax.random.randint(main_key, (TILES, P_MAX), 0, TX)
    last_row = jax.random.randint(last_key, (P_MAX,), 0, TX - WIN + 1)
    offsets = offsets.at[TILES - 1].set(last_row)
    offsets = offsets.at[0, 0].set(TX - 1)
    offsets = offsets.at[1, 0].set(0)
    return offsets.reshape(POSITIONS).astype(jnp.int32)


def draw_col_offset(key, part):
    offsets = jax.random.randint(key, (TILES, P_MAX), 0, TY - WIN + 1)
    offsets = offsets.at[0, 0].set(TY - WIN)
    offsets = offsets.at[1, 0].set(0)
    return offsets.reshape(POSITIONS).astype(jnp.int32)


def draw_tile_counts(key, part):
    first_key, second_key, heavy_key = jax.random.split(key, 3)
    first_draw = jax.random.randint(first_key, (TILES,), 1, P_MAX + 1)
    second_draw = jax.random.randint(second_key, (TILES,), 1, P_MAX + 1)
    counted = jnp.minimum(first_draw, second_draw)
    heavy_tile = jax.random.randint(heavy_key, (), 0, TILES)
    counted = counted.at[heavy_tile].set(P_MAX)
    counted = counted.at[(heavy_tile + 1) % TILES].set(1)
    return counted.astype(jnp.int32)


def shard_levels(key, extent, cuts, least, largest):
    def one(dim, shards_of):
        steps = jax.random.uniform(jax.random.fold_in(jax.random.fold_in(key, 6), dim), (shards_of,), jnp.float32, least / len(cuts), largest / len(cuts))
        return jnp.repeat(jnp.exp(steps), extent[dim] // shards_of).reshape((-1,) + (1,) * (len(extent) - dim - 1))

    factor_of = one(*cuts[0])
    for cut in cuts[1:]:
        factor_of = factor_of * one(*cut)
    return factor_of


def gaussian(stream_key, extent, spread, limit, kind=jnp.bfloat16):
    values = spread * jax.random.normal(stream_key, extent, jnp.float32)
    return jnp.clip(values, min=-limit, max=limit).astype(kind)


def setup_inputs(seed: int = 0, part: int = 0) -> dict:
    key_of = jax.random.split(jax.random.key(seed), 7)
    part_splits = jax.random.split(jax.random.fold_in(key_of[6], part), 7)
    return {
        "object_field": draw_object_field(jax.random.fold_in(jax.random.fold_in(key_of[6], part), 71), part),
        "probe_modes": gaussian(part_splits[1], (MODES, 2, WIN, WIN), 0.35, 2.1, jnp.float32),
        "measured": jnp.clip(2.0 * jax.random.uniform(part_splits[2], (POSITIONS, WIN, WIN), jnp.float32) ** shard_levels(part_splits[2], (POSITIONS, WIN, WIN), ((0, 16),), -0.2, 0.2), 0.0, 2.0),
        "row_offset": draw_row_offset(jax.random.fold_in(jax.random.fold_in(key_of[6], part), 71), part),
        "col_offset": draw_col_offset(jax.random.fold_in(jax.random.fold_in(key_of[6], part), 71), part),
        "tile_counts": draw_tile_counts(jax.random.fold_in(jax.random.fold_in(key_of[6], part), 71), part),
    }


def make_tables(width):
    index = jnp.arange(width).astype(jnp.int32)
    product = index[:, None] * index[None, :] % width
    phase_angle = 2.0 * math.pi / width * product.astype(jnp.float32)
    scale_norm = 1.0 / math.sqrt(width)
    dft_re = jnp.cos(phase_angle) * scale_norm
    dft_im = -jnp.sin(phase_angle) * scale_norm
    frequency = jnp.where(index < width // 2, index, index - width).astype(jnp.float32)
    phase_map = -0.5 * math.pi / width * (frequency[:, None] ** 2 + frequency[None, :] ** 2)
    return (dft_re, dft_im, jnp.cos(phase_map), jnp.sin(phase_map))

def matmul_high(left, right):
    return jnp.matmul(left, right, precision=lax.Precision.HIGHEST)

def transform(wave_re, wave_im, dft_re, dft_im):
    first_re = matmul_high(wave_re, dft_re) - matmul_high(wave_im, dft_im)
    first_im = matmul_high(wave_re, dft_im) + matmul_high(wave_im, dft_re)
    second_re = matmul_high(dft_re, first_re) - matmul_high(dft_im, first_im)
    second_im = matmul_high(dft_re, first_im) + matmul_high(dft_im, first_re)
    return (second_re, second_im)

def position_loss(obj_patch, modes_in, pattern, tables_four):
    dft_re, dft_im, prop_re, prop_im = tables_four
    obj_re, obj_im = (obj_patch[0, 0], obj_patch[0, 1])
    wave_re = modes_in[:, 0] * obj_re - modes_in[:, 1] * obj_im
    wave_im = modes_in[:, 0] * obj_im + modes_in[:, 1] * obj_re
    for slice_idx in range(1, obj_patch.shape[0]):
        spec_re, spec_im = transform(wave_re, wave_im, dft_re, dft_im)
        moved_re = spec_re * prop_re - spec_im * prop_im
        moved_im = spec_re * prop_im + spec_im * prop_re
        back_re, back_im = transform(moved_re, moved_im, dft_re, -dft_im)
        obj_re, obj_im = (obj_patch[slice_idx, 0], obj_patch[slice_idx, 1])
        wave_re = back_re * obj_re - back_im * obj_im
        wave_im = back_re * obj_im + back_im * obj_re
    far_re, far_im = transform(wave_re, wave_im, dft_re, dft_im)
    intensity = lax.optimization_barrier(jnp.sum(far_re * far_re + far_im * far_im, axis=0))
    residue_map = intensity - pattern
    return 0.5 * jnp.sum(residue_map * residue_map)

def reference(object_field, probe_modes, measured, row_offset, col_offset, tile_counts):
    tables_four = make_tables(WIN)
    total_rows = TILES * TX
    padded = jnp.pad(object_field, ((0, 0), (0, 0), (0, WIN), (0, 0)))
    slot_ids = jnp.arange(POSITIONS).astype(jnp.int32)
    owner_tile = slot_ids // P_MAX
    live_mask = (slot_ids % P_MAX < tile_counts[owner_tile]).astype(jnp.float32)
    start_rows = (owner_tile * TX + row_offset).astype(jnp.int32)
    start_cols = col_offset.astype(jnp.int32)
    probe_power = lax.optimization_barrier(jnp.sum(probe_modes * probe_modes, axis=(0, 1)))
    zero_idx = jnp.zeros((), jnp.int32)

    def visit(state_now, inputs):
        grad_obj, illumination, grad_probe, obj_power = state_now
        start_row, start_col, weight, pattern = inputs
        corner = (zero_idx, zero_idx, start_row, start_col)
        obj_patch = lax.dynamic_slice(padded, corner, (SLICES, 2, WIN, WIN))

        def loss_of(patch_in, modes_in):
            return position_loss(patch_in, modes_in, pattern, tables_four)
        loss_value, pullback = jax.vjp(loss_of, obj_patch, probe_modes)
        grad_patch, grad_modes = pullback(weight.astype(loss_value.dtype))
        current = lax.dynamic_slice(grad_obj, corner, (SLICES, 2, WIN, WIN))
        grad_obj = lax.dynamic_update_slice(grad_obj, current + grad_patch, corner)
        lit_now = lax.dynamic_slice(illumination, (start_row, start_col), (WIN, WIN))
        illumination = lax.dynamic_update_slice(illumination, lit_now + weight * probe_power, (start_row, start_col))
        grad_probe = grad_probe + grad_modes
        obj_power = obj_power + weight * (obj_patch[0, 0] ** 2 + obj_patch[0, 1] ** 2)
        return ((grad_obj, illumination, grad_probe, obj_power), None)
    initial = (jnp.zeros(padded.shape, jnp.float32), jnp.zeros((total_rows + WIN, TY), jnp.float32), jnp.zeros(probe_modes.shape, jnp.float32), jnp.zeros((WIN, WIN), jnp.float32))
    final_state, _ = lax.scan(visit, initial, (start_rows, start_cols, live_mask, measured))
    grad_obj, illumination, grad_probe, obj_power = final_state
    updated_object = object_field - 0.5 * grad_obj[:, :, :total_rows] / (illumination[:total_rows] + 1.0)
    updated_probe = probe_modes - 0.5 * grad_probe / (obj_power + 1.0)
    return (updated_object, updated_probe)
```

```python
import functools
import math

import jax
import jax.numpy as jnp
import ml_dtypes
import numpy as np
from jax import lax
from jax.experimental import pallas as pl
from jax.experimental.pallas import tpu as pltpu
from jax.sharding import PartitionSpec as P

F32, BF16 = jnp.float32, jnp.bfloat16


def passed_along(value, axis, steps):
    count = lax.axis_size(axis)
    leading, last = (max(0, -steps), min(count, count - steps))
    return lax.ppermute(value, axis, [(source, source + steps) for source in range(leading, last)])


def complex_tables(width):
    index = np.arange(width)
    angle = 2.0 * math.pi / width * (index[:, None] * index[None, :] % width)
    dft = np.exp(-1j * angle) / math.sqrt(width)
    frequency = np.where(index < width // 2, index, index - width).astype(np.float64)
    phase = np.exp(-0.5j * math.pi / width * frequency**2)
    return dft, np.conj(dft) @ (phase[:, None] * dft)


def real_forms(table):
    re, im = table.real, table.imag
    right = np.block([[re, im], [-im, re]])
    left = np.block([[re, -im], [im, re]])

    def parts(matrix):
        high = matrix.astype(ml_dtypes.bfloat16)
        low = (matrix - high.astype(np.float64)).astype(ml_dtypes.bfloat16)
        return high, low

    right_high, right_low = parts(right)
    left_high, left_low = parts(left)
    return np.stack([right_high, right_low]), np.concatenate([left_high, left_low], 0)


def halves(value):
    high = value.astype(BF16)
    return high, (value - high.astype(F32)).astype(BF16)


def dot(left, right):
    return jnp.dot(left, right, preferred_element_type=F32)


def two_sided(blocks, right_ref, left_ref):
    modes, width = len(blocks), blocks[0][0].shape[0]
    rows = jnp.concatenate([jnp.concatenate(pair, 1) for pair in blocks], 0)
    high, low = halves(rows)
    both = dot(jnp.concatenate([high, low], 0), right_ref[0])
    first = both[: modes * width] + both[modes * width :] + dot(high, right_ref[1])
    cols = jnp.concatenate(
        [
            jnp.concatenate(
                [first[m * width : (m + 1) * width, part * width : (part + 1) * width] for m in range(modes)], 1
            )
            for part in range(2)
        ],
        0,
    )
    high, low = halves(cols)
    both = dot(left_ref[...], high)
    second = both[: 2 * width] + both[2 * width :] + dot(left_ref[: 2 * width], low)
    return [
        (second[:width, m * width : (m + 1) * width], second[width:, m * width : (m + 1) * width])
        for m in range(modes)
    ]


def times(left, right):
    return left[0] * right[0] - left[1] * right[1], left[0] * right[1] + left[1] * right[0]


def window_place(row_start, col_start, width, blocks):
    block = col_start // width
    shift = col_start - block * width
    lane = lax.broadcasted_iota(jnp.int32, (width, width), 1)
    row = lax.broadcasted_iota(jnp.int32, (width, width), 0)
    first = pl.ds(pl.multiple_of(block * width, width), width)
    second = pl.ds(pl.multiple_of(jnp.minimum(block + 1, blocks - 1) * width, width), width)
    return row >= row_start, lane >= shift, shift, first, second


def gradient_kernel(
    place_ref, object_ref, rim_ref, probe_ref, measured_ref, fr_ref, fl_ref, pr_ref, pl_ref,
    own_ref, next_ref, sums_ref,
):
    slices, _, _, tile_cols = object_ref.shape
    modes, _, width, _ = probe_ref.shape
    slots = measured_ref.shape[0]
    own_ref[...] = jnp.zeros(own_ref.shape, F32)
    next_ref[...] = jnp.zeros(next_ref.shape, F32)
    sums_ref[...] = jnp.zeros(sums_ref.shape, F32)

    def visit(slot, carry):
        row_start, col_start = place_ref[1 + slot], place_ref[1 + slots + slot]
        in_own, in_first, shift, first, second = window_place(row_start, col_start, width, tile_cols // width)

        def window(s, part):
            own = jnp.where(in_first, object_ref[s, part, :, first], object_ref[s, part, :, second])
            rim = jnp.where(in_first, rim_ref[s, part, :, first], rim_ref[s, part, :, second])
            stored = jnp.where(in_own, own, rim)
            stored = pltpu.roll(stored, lax.rem(width - row_start, width), 0)
            return pltpu.roll(stored, lax.rem(width - shift, width), 1)

        def put(s, part, value):
            value = pltpu.roll(pltpu.roll(value, row_start, 0), shift, 1)
            zero = jnp.zeros_like(value)
            own, rim = jnp.where(in_own, value, zero), jnp.where(in_own, zero, value)
            own_ref[s, part, :, first] += jnp.where(in_first, own, zero)
            own_ref[s, part, :, second] += jnp.where(in_first, zero, own)
            next_ref[s, part, :, first] += jnp.where(in_first, rim, zero)
            next_ref[s, part, :, second] += jnp.where(in_first, zero, rim)

        layer_one = (window(0, 0), window(0, 1))
        layer_two = (window(1, 0), window(1, 1))
        probe = [(probe_ref[m, 0], probe_ref[m, 1]) for m in range(modes)]
        moved = two_sided([times(p, layer_one) for p in probe], pr_ref, pl_ref)
        far = two_sided([times(w, layer_two) for w in moved], fr_ref, fl_ref)
        intensity = sum(re * re + im * im for re, im in far)
        residue = 2.0 * (intensity - measured_ref[slot])
        back = two_sided([(residue * re, -(residue * im)) for re, im in far], fr_ref, fl_ref)
        terms = [times(w, g) for w, g in zip(moved, back)]
        put(1, 0, sum(t[0] for t in terms))
        put(1, 1, -sum(t[1] for t in terms))
        back = two_sided([times(g, layer_two) for g in back], pr_ref, pl_ref)
        terms = [times(p, g) for p, g in zip(probe, back)]
        put(0, 0, sum(t[0] for t in terms))
        put(0, 1, -sum(t[1] for t in terms))
        for m in range(modes):
            grad = times(layer_one, back[m])
            sums_ref[2 * m] += grad[0]
            sums_ref[2 * m + 1] -= grad[1]
        sums_ref[2 * modes] += layer_one[0] * layer_one[0] + layer_one[1] * layer_one[1]
        return carry

    lax.fori_loop(0, place_ref[0], visit, 0)


def illumination_kernel(place_ref, before_ref, probe_ref, lit_ref):
    tile_cols = lit_ref.shape[1]
    modes, _, width, _ = probe_ref.shape
    slots = (place_ref.shape[0] - 1) // 2
    lit_ref[...] = jnp.zeros(lit_ref.shape, F32)
    power = sum(probe_ref[m, part] * probe_ref[m, part] for m in range(modes) for part in range(2))

    def add(slot, ref, own):
        row_start, col_start = ref[1 + slot], ref[1 + slots + slot]
        in_own, in_first, shift, first, second = window_place(row_start, col_start, width, tile_cols // width)
        value = pltpu.roll(pltpu.roll(power, row_start, 0), shift, 1)
        zero = jnp.zeros_like(value)
        value = jnp.where(in_own, value, zero) if own else jnp.where(in_own, zero, value)
        lit_ref[:, first] += jnp.where(in_first, value, zero)
        lit_ref[:, second] += jnp.where(in_first, zero, value)

    @pl.loop(0, place_ref[0])
    def _(slot):
        add(slot, place_ref, True)

    @pl.loop(0, before_ref[0])
    def _(slot):
        add(slot, before_ref, False)


def all_sum(value, axis):
    count = lax.axis_size(axis)
    index = lax.axis_index(axis)
    bits = [1 << b for b in range(count.bit_length() - 1)]
    halved = []
    for bit in bits:
        pairs = [(i, i ^ bit) for i in range(count)]
        low_side = (index // bit) % 2 == 0
        half = value.shape[0] // 2
        if len(halved) < 3:
            low, high = value[:half], value[half:]
            kept, sent = jnp.where(low_side, low, high), jnp.where(low_side, high, low)
            value = kept + lax.ppermute(sent, axis, pairs)
            halved.append((pairs, low_side))
        else:
            value = value + lax.ppermute(value, axis, pairs)
    for pairs, low_side in reversed(halved):
        got = lax.ppermute(value, axis, pairs)
        value = jnp.concatenate([jnp.where(low_side, value, got), jnp.where(low_side, got, value)], 0)
    return value


def body(object_field, probe_modes, measured, row_offset, col_offset, tile_counts):
    slices, _, tile_rows, tile_cols = object_field.shape
    modes, _, width, _ = probe_modes.shape
    dft, move = complex_tables(width)
    tables = [jnp.asarray(t) for t in (*real_forms(dft), *real_forms(move))]
    tile_idx = lax.axis_index("tile")
    counts = lax.dynamic_slice(jnp.concatenate([jnp.zeros((1,), jnp.int32), tile_counts]), (tile_idx,), (2,))
    place = jnp.concatenate([counts[1:], row_offset, col_offset])
    before = passed_along(place, "tile", 1)
    rim_rows = passed_along(object_field, "tile", -1)
    smem = pl.BlockSpec(memory_space=pltpu.SMEM)
    vmem = pl.BlockSpec(memory_space=pltpu.VMEM)
    params = pltpu.CompilerParams(vmem_limit_bytes=56 << 20)
    illumination = pl.pallas_call(
        illumination_kernel,
        out_shape=jax.ShapeDtypeStruct((tile_rows, tile_cols), F32),
        in_specs=[smem, smem, vmem],
        out_specs=vmem,
        compiler_params=params,
    )(place, before, probe_modes)
    grad_own, grad_next, sums = pl.pallas_call(
        gradient_kernel,
        out_shape=(
            jax.ShapeDtypeStruct(object_field.shape, F32),
            jax.ShapeDtypeStruct((slices, 2, width, tile_cols), F32),
            jax.ShapeDtypeStruct((2 * modes + 1, width, width), F32),
        ),
        in_specs=[smem] + [vmem] * 8,
        out_specs=(vmem,) * 3,
        compiler_params=params,
    )(place, object_field, rim_rows, probe_modes, measured, *tables)
    arrived = passed_along(grad_next, "tile", 1)
    total = all_sum(sums.reshape(-1, width), "tile").reshape(sums.shape)
    updated_object = object_field - 0.5 * (grad_own + arrived) / (illumination + 1.0)
    grad_total = total[: 2 * modes].reshape(probe_modes.shape)
    updated_probe = probe_modes - 0.5 * grad_total / (total[2 * modes] + 1.0)
    return (updated_object, updated_probe)


def solution(mesh):
    return jax.shard_map(
        body,
        mesh=mesh,
        in_specs=(
            P("groups", None, "tile", None),
            P("groups", None, None, None),
            P(("groups", "tile"), None, None),
            P(("groups", "tile")),
            P(("groups", "tile")),
            P("groups"),
        ),
        out_specs=(P("groups", None, "tile", None), P("groups", None, None, None)),
        check_vma=False,
    )
```

```python
import functools
import math

import jax
import jax.numpy as jnp
import ml_dtypes
import numpy as np
from jax import lax
from jax.experimental import pallas as pl
from jax.experimental.pallas import tpu as pltpu
from jax.sharding import PartitionSpec as P

F32, BF16 = jnp.float32, jnp.bfloat16


def passed_along(value, axis, steps):
    count = lax.axis_size(axis)
    leading, last = (max(0, -steps), min(count, count - steps))
    return lax.ppermute(value, axis, [(source, source + steps) for source in range(leading, last)])


def complex_tables(width):
    index = np.arange(width)
    angle = 2.0 * math.pi / width * (index[:, None] * index[None, :] % width)
    dft = np.exp(-1j * angle) / math.sqrt(width)
    frequency = np.where(index < width // 2, index, index - width).astype(np.float64)
    phase = np.exp(-0.5j * math.pi / width * frequency**2)
    return dft, np.conj(dft) @ (phase[:, None] * dft)


def real_forms(table):
    re, im = table.real, table.imag
    right = np.block([[re, im], [-im, re]])
    left = np.block([[re, -im], [im, re]])

    def parts(matrix):
        high = matrix.astype(ml_dtypes.bfloat16)
        low = (matrix - high.astype(np.float64)).astype(ml_dtypes.bfloat16)
        return high, low

    right_high, right_low = parts(right)
    left_high, left_low = parts(left)
    return np.stack([right_high, right_low]), np.concatenate([left_high, left_low], 0)


def halves(value):
    high = value.astype(BF16)
    return high, (value - high.astype(F32)).astype(BF16)


def dot(left, right):
    return jnp.dot(left, right, preferred_element_type=F32)


def right_stage(blocks, right_ref):
    rows = jnp.concatenate([jnp.concatenate(pair, 1) for pair in blocks], 0)
    high, low = halves(rows)
    table = jnp.concatenate([right_ref[0], right_ref[0], right_ref[1]], 0)
    return dot(jnp.concatenate([high, low, high], 1), table)


def left_stage(first, width, left_ref):
    modes = first.shape[0] // width
    cols = jnp.concatenate(
        [
            jnp.concatenate(
                [first[m * width : (m + 1) * width, part * width : (part + 1) * width] for m in range(modes)], 1
            )
            for part in range(2)
        ],
        0,
    )
    high, low = halves(cols)
    table = jnp.concatenate([left_ref[: 2 * width], left_ref[: 2 * width], left_ref[2 * width :]], 1)
    second = dot(table, jnp.concatenate([high, low, high], 0))
    return [
        (second[:width, m * width : (m + 1) * width], second[width:, m * width : (m + 1) * width])
        for m in range(modes)
    ]


def two_sided(blocks, right_ref, left_ref, group=2):
    width = blocks[0][0].shape[0]
    firsts = [right_stage(blocks[i : i + group], right_ref) for i in range(0, len(blocks), group)]
    return [block for first in firsts for block in left_stage(first, width, left_ref)]


def times(left, right):
    return left[0] * right[0] - left[1] * right[1], left[0] * right[1] + left[1] * right[0]


def window_place(place_ref, slot, slots, width, blocks):
    row_start, col_start = place_ref[slot], place_ref[slots + slot]
    block = col_start // width
    shift = col_start - block * width
    lane = lax.broadcasted_iota(jnp.int32, (width, width), 1)
    row = lax.broadcasted_iota(jnp.int32, (width, width), 0)
    first = pl.ds(pl.multiple_of(block * width, width), width)
    second = pl.ds(pl.multiple_of(jnp.minimum(block + 1, blocks - 1) * width, width), width)
    return row >= row_start, lane >= shift, shift, first, second


def load_kernel(*refs):
    count = len(refs) // 2
    for source, target in zip(refs[:count], refs[count:]):
        target[...] = source[...]


def strip_kernel(start, before_ref, object_ref, strip_ref):
    size, planes, width, _ = strip_ref.shape
    slots = before_ref.shape[0] // 2
    for i in range(size):
        _, in_first, _, first, second = window_place(before_ref, start + i, slots, width, object_ref.shape[-1] // width)
        for plane in range(planes):
            strip_ref[i, plane] = jnp.where(
                in_first, object_ref[plane // 2, plane % 2, :, first], object_ref[plane // 2, plane % 2, :, second]
            )


PAIR = 2


def gradient_kernel(
    start, axis, counts_ref, place_ref, object_ref, probe_ref, measured_ref, fr_ref, fl_ref, pr_ref, pl_ref, *refs
):
    last_call = start > 0
    tile = lax.axis_index(axis)
    count = counts_ref[tile]
    modes, _, width, _ = probe_ref.shape
    slots = measured_ref.shape[0]
    rim_refs, refs = refs[: 1 + last_call], refs[1 + last_call :]
    rims = [(ref, i) for ref in rim_refs for i in range(ref.shape[0])]
    if last_call:
        before_ref, grad_ref, kept_ref, sent_ref, sums_ref = refs
        sums_ref[...] = before_ref[...]
    else:
        grad_ref, sums_ref = refs
        sums_ref[...] = jnp.zeros(sums_ref.shape, F32)
    probe = [(probe_ref[m, 0], probe_ref[m, 1]) for m in range(modes)]

    def visit(base):
        places = [
            window_place(place_ref, start + base + i, slots, width, object_ref.shape[-1] // width) for i in range(PAIR)
        ]

        def window(i, s, part):
            in_own, in_first, shift, first, second = places[i]
            own = jnp.where(in_first, object_ref[s, part, :, first], object_ref[s, part, :, second])
            rim_ref, at = rims[start + base + i]
            stored = jnp.where(in_own, own, rim_ref[at, 2 * s + part])
            stored = pltpu.roll(stored, lax.rem(width - place_ref[start + base + i], width), 0)
            return pltpu.roll(stored, lax.rem(width - shift, width), 1)

        def put(i, s, part, value):
            value = pltpu.roll(value, place_ref[start + base + i], 0)
            grad_ref[base + i, 2 * s + part] = pltpu.roll(value, places[i][2], 1)

        def split(blocks):
            return [blocks[i * modes : (i + 1) * modes] for i in range(PAIR)]

        ones = [(window(i, 0, 0), window(i, 0, 1)) for i in range(PAIR)]
        moved = split(two_sided([times(p, one) for one in ones for p in probe], pr_ref, pl_ref))
        twos = [(window(i, 1, 0), window(i, 1, 1)) for i in range(PAIR)]
        far = split(two_sided([times(w, two) for ws, two in zip(moved, twos) for w in ws], fr_ref, fl_ref))
        back = []
        for i in range(PAIR):
            intensity = sum(re * re + im * im for re, im in far[i])
            residue = 2.0 * (intensity - measured_ref[start + base + i])
            back += [(residue * re, -(residue * im)) for re, im in far[i]]
        back = split(two_sided(back, fr_ref, fl_ref))
        last = split(two_sided([times(g, two) for gs, two in zip(back, twos) for g in gs], pr_ref, pl_ref))
        for i in range(PAIR):
            terms = [times(w, g) for w, g in zip(moved[i], back[i])]
            put(i, 1, 0, sum(t[0] for t in terms))
            put(i, 1, 1, -sum(t[1] for t in terms))
            terms = [times(p, g) for p, g in zip(probe, last[i])]
            put(i, 0, 0, sum(t[0] for t in terms))
            put(i, 0, 1, -sum(t[1] for t in terms))
        live = [start + base + i < count for i in range(PAIR)]

        def summed(values):
            return sum(jnp.where(alive, value, 0.0) for alive, value in zip(live, values))

        for m in range(modes):
            grads = [times(one, g[m]) for one, g in zip(ones, last)]
            for part, sign in ((0, 1.0), (1, -1.0)):
                rows = pl.ds((2 * m + part) * width, width)
                sums_ref[rows] += sign * summed(g[part] for g in grads)
        sums_ref[pl.ds(2 * modes * width, width)] += summed(re * re + im * im for re, im in ones)

    for base in range(0, grad_ref.shape[0], PAIR):
        pl.when(start + base < count)(functools.partial(visit, base))
    if last_call:
        half = kept_ref.shape[0]
        side = lax.rem(tile, 2)
        kept_ref[...] = sums_ref[pl.ds(pl.multiple_of(side * half, 8), half)]
        sent_ref[...] = sums_ref[pl.ds(pl.multiple_of((1 - side) * half, 8), half)]


def add_windows(target_ref, counts_ref, place_ref, before_ref, axis, window_of):
    tile = lax.axis_index(axis)
    width, slots = target_ref.shape[0], place_ref.shape[0] // 2
    target_ref[...] = jnp.zeros(target_ref.shape, F32)
    for slot in range(slots):
        for own in (True, False):
            ref = place_ref if own else before_ref
            count = counts_ref[tile] if own else jnp.where(tile > 0, counts_ref[jnp.maximum(tile - 1, 0)], 0)

            @pl.when(slot < count)
            def _():
                in_own, in_first, shift, first, second = window_place(
                    ref, slot, slots, width, target_ref.shape[1] // width
                )
                value = window_of(ref, slot, own, shift)
                wanted = in_own if own else jnp.logical_not(in_own)
                value = jnp.where(wanted, value, 0.0)
                target_ref[:, first] += jnp.where(in_first, value, 0.0)
                target_ref[:, second] += jnp.where(in_first, 0.0, value)


def light_kernel(axis, counts_ref, place_ref, before_ref, probe_ref, lit_ref):
    modes = probe_ref.shape[0]
    power = sum(probe_ref[m, part] * probe_ref[m, part] for m in range(modes) for part in range(2))

    def window_of(ref, slot, own, shift):
        return pltpu.roll(pltpu.roll(power, ref[slot], 0), shift, 1)

    add_windows(lit_ref, counts_ref, place_ref, before_ref, axis, window_of)
    lit_ref[...] = 0.5 / (lit_ref[...] + 1.0)


def update_kernel(axis, sizes, counts_ref, place_ref, before_ref, object_ref, lit_ref, *refs):
    out_ref, sum_ref = refs[2 * len(sizes) :]
    plane = pl.program_id(0)
    parts = [(n, i) for n, size in enumerate(sizes) for i in range(size)]

    def window_of(ref, slot, own, shift):
        n, i = parts[slot]
        return refs[n + (0 if own else len(sizes))][i, plane]

    add_windows(sum_ref, counts_ref, place_ref, before_ref, axis, window_of)
    out_ref[0, 0] = object_ref[plane // 2, plane % 2] - sum_ref[...] * lit_ref[...]


def probe_kernel(axis, mine_ref, got_ref, probe_ref, out_ref, total_ref):
    modes, _, width, _ = probe_ref.shape
    half = mine_ref.shape[0]
    side = lax.rem(lax.axis_index(axis), 2)
    total_ref[pl.ds(pl.multiple_of(side * half, 8), half)] = mine_ref[...]
    total_ref[pl.ds(pl.multiple_of((1 - side) * half, 8), half)] = got_ref[...]
    scale = 0.5 / (total_ref[pl.ds(2 * modes * width, width)] + 1.0)
    for m in range(modes):
        for part in range(2):
            out_ref[m, part] = probe_ref[m, part] - total_ref[pl.ds((2 * m + part) * width, width)] * scale


def after(value, *others):
    return lax.optimization_barrier((value, *others))[0]


def halve_kernel(axis, bit, kept_ref, got_ref, next_kept_ref, next_sent_ref):
    half = next_kept_ref.shape[0]
    side = lax.rem(lax.axis_index(axis) // bit, 2)
    for ref, which in ((next_kept_ref, side), (next_sent_ref, 1 - side)):
        rows = pl.ds(pl.multiple_of(which * half, 8), half)
        ref[...] = kept_ref[rows] + got_ref[rows]


def add_kernel(kept_ref, got_ref, out_ref):
    out_ref[...] = kept_ref[...] + got_ref[...]


def join_kernel(axis, bit, mine_ref, got_ref, out_ref):
    half = mine_ref.shape[0]
    side = lax.rem(lax.axis_index(axis) // bit, 2)
    out_ref[pl.ds(pl.multiple_of(side * half, 8), half)] = mine_ref[...]
    out_ref[pl.ds(pl.multiple_of((1 - side) * half, 8), half)] = got_ref[...]


def half_sum(kept, sent, axis, beside, joins):
    count = lax.axis_size(axis)
    bits = [1 << b for b in range(count.bit_length() - 1)]
    vmem = pl.BlockSpec(memory_space=pltpu.VMEM)
    width = kept.shape[1]

    def exchanged(value, bit, step):
        value = after(value, *joins.get(step, ()))
        got = lax.ppermute(value, axis, [(i, i ^ bit) for i in range(count)])
        beside.get(step, lambda reached: None)(got)
        return pltpu.with_memory_space_constraint(got, pltpu.VMEM)

    def local(kernel, rows, *operands):
        return pl.pallas_call(
            kernel,
            out_shape=[pltpu.VMEM((n, width), F32) for n in rows],
            in_specs=[vmem] * 2,
            out_specs=[vmem] * len(rows),
            compiler_params=pltpu.CompilerParams(vmem_limit_bytes=4 << 20),
        )(*operands)

    got = exchanged(sent, bits[0], 0)
    halved = bits[1:3]
    for step, bit in enumerate(bits[1:], 1):
        rows = kept.shape[0]
        if bit in halved:
            kept, sent = local(functools.partial(halve_kernel, axis, bit), (rows // 2,) * 2, kept, got)
        else:
            (kept,) = local(add_kernel, (rows,), kept, got)
            sent = kept
        got = exchanged(sent, bit, step)
    (value,) = local(add_kernel, kept.shape[:1], kept, got)
    for step, bit in enumerate(reversed(halved), len(bits)):
        got = exchanged(value, bit, step)
        (value,) = local(functools.partial(join_kernel, axis, bit), (2 * value.shape[0],), value, got)
    return value, exchanged(value, bits[0], len(bits) + len(halved))


def body(object_field, probe_modes, measured, row_offset, col_offset, tile_counts):
    axis = "tile"
    slices, _, tile_rows, tile_cols = object_field.shape
    modes, _, width, _ = probe_modes.shape
    slots = measured.shape[0]
    dft, move = complex_tables(width)
    smem = pl.BlockSpec(memory_space=pltpu.SMEM)
    vmem = pl.BlockSpec(memory_space=pltpu.VMEM)
    params = pltpu.CompilerParams(vmem_limit_bytes=16 << 20)

    def held(value):
        return pltpu.with_memory_space_constraint(value, pltpu.VMEM)

    def held_like(value):
        return pltpu.VMEM(value.shape, value.dtype)

    place = jnp.concatenate([row_offset, col_offset])
    before = passed_along(place, axis, 1)
    loaded = [jnp.asarray(t) for t in (*real_forms(dft), *real_forms(move))]
    loaded = [object_field, probe_modes, measured, *loaded]
    objects, probe, patterns, *tables = pl.pallas_call(
        load_kernel,
        out_shape=tuple(map(held_like, loaded)),
        in_specs=[vmem] * len(loaded),
        out_specs=(vmem,) * len(loaded),
        compiler_params=params,
    )(*loaded)
    sizes = (PAIR, slots - PAIR)

    def windows(size):
        return pltpu.VMEM((size, 2 * slices, width, width), F32)

    rims, strip = [], before
    for start, size in ((0, slots // 2), (slots // 2, slots - slots // 2)):
        strip = pl.pallas_call(
            functools.partial(strip_kernel, start),
            out_shape=windows(size),
            in_specs=[smem, vmem],
            out_specs=vmem,
            compiler_params=params,
        )(after(before, strip), objects)
        rims.append(held(passed_along(strip, axis, -1)))
    lit = pl.pallas_call(
        functools.partial(light_kernel, axis),
        out_shape=pltpu.VMEM((tile_rows, tile_cols), F32),
        in_specs=[smem, smem, smem, vmem],
        out_specs=vmem,
        compiler_params=params,
    )(tile_counts, place, after(before, strip), probe)
    rows = (2 * modes + 1) * width
    whole, half = pltpu.VMEM((rows, width), F32), pltpu.VMEM((rows // 2, width), F32)
    common = (probe, patterns, *tables)
    grad_a, sums = pl.pallas_call(
        functools.partial(gradient_kernel, 0, axis),
        out_shape=(windows(sizes[0]), whole),
        in_specs=[smem] * 2 + [vmem] * 8,
        out_specs=(vmem,) * 2,
        compiler_params=params,
    )(tile_counts, after(place, lit), objects, *common, rims[0])
    arrived_a = passed_along(grad_a, axis, 1)
    grad_b, kept, sent = pl.pallas_call(
        functools.partial(gradient_kernel, sizes[0], axis),
        out_shape=(windows(sizes[1]), half, half),
        in_specs=[smem] * 2 + [vmem] * 10,
        out_specs=(vmem,) * 3,
        scratch_shapes=[whole],
        compiler_params=params,
        cost_estimate=pl.CostEstimate(flops=1, bytes_accessed=40 << 20, transcendentals=0),
    )(tile_counts, place, objects, *common, *rims, sums)
    arrived = [arrived_a]

    def send_rest(reached):
        arrived.append(passed_along(after(grad_b, reached), axis, 1))

    mine, got = half_sum(kept, sent, axis, {1: send_rest}, {1: arrived[:1], 5: arrived})
    updated_object = pl.pallas_call(
        functools.partial(update_kernel, axis, sizes),
        grid=(2 * slices,),
        out_shape=jax.ShapeDtypeStruct(object_field.shape, F32),
        in_specs=[smem] * 3 + [vmem] * 6,
        out_specs=pl.BlockSpec((1, 1, tile_rows, tile_cols), lambda plane: (plane // 2, plane % 2, 0, 0)),
        scratch_shapes=[pltpu.VMEM((tile_rows, tile_cols), F32)],
        compiler_params=params,
        cost_estimate=pl.CostEstimate(flops=1, bytes_accessed=12 << 20, transcendentals=0),
    )(tile_counts, place, before, objects, lit, grad_a, grad_b, *map(held, arrived))
    updated_probe = pl.pallas_call(
        functools.partial(probe_kernel, axis),
        out_shape=jax.ShapeDtypeStruct(probe_modes.shape, F32),
        in_specs=[vmem] * 3,
        out_specs=vmem,
        scratch_shapes=[pltpu.VMEM((rows, width), F32)],
        compiler_params=params,
    )(mine, got, probe)
    return (updated_object, updated_probe)


def solution(mesh):
    return jax.shard_map(
        body,
        mesh=mesh,
        in_specs=(
            P("groups", None, "tile", None),
            P("groups", None, None, None),
            P(("groups", "tile"), None, None),
            P(("groups", "tile")),
            P(("groups", "tile")),
            P("groups"),
        ),
        out_specs=(P("groups", None, "tile", None), P("groups", None, None, None)),
        check_vma=False,
    )
```

```python
import functools
import math

import jax
import jax.numpy as jnp
import ml_dtypes
import numpy as np
from jax import lax
from jax.experimental import pallas as pl
from jax.experimental.pallas import tpu as pltpu
from jax.sharding import PartitionSpec as P

F32, BF16 = jnp.float32, jnp.bfloat16


def passed_along(value, axis, steps):
    count = lax.axis_size(axis)
    leading, last = (max(0, -steps), min(count, count - steps))
    return lax.ppermute(value, axis, [(source, source + steps) for source in range(leading, last)])


def complex_tables(width):
    index = np.arange(width)
    angle = 2.0 * math.pi / width * (index[:, None] * index[None, :] % width)
    dft = np.exp(-1j * angle) / math.sqrt(width)
    frequency = np.where(index < width // 2, index, index - width).astype(np.float64)
    phase = np.exp(-0.5j * math.pi / width * frequency**2)
    return dft, np.conj(dft) @ (phase[:, None] * dft)


def real_forms(table):
    re, im = table.real, table.imag
    right = np.block([[re, im], [-im, re]])
    left = np.block([[re, -im], [im, re]])

    def parts(matrix):
        high = matrix.astype(ml_dtypes.bfloat16)
        low = (matrix - high.astype(np.float64)).astype(ml_dtypes.bfloat16)
        return high, low

    right_high, right_low = parts(right)
    left_high, left_low = parts(left)
    return np.stack([right_high, right_low]), np.concatenate([left_high, left_low], 0)


def halves(value):
    high = value.astype(BF16)
    return high, (value - high.astype(F32)).astype(BF16)


def dot(left, right):
    return jnp.dot(left, right, preferred_element_type=F32)


def right_stage(blocks, right_ref):
    rows = jnp.concatenate([jnp.concatenate(pair, 1) for pair in blocks], 0)
    high, low = halves(rows)
    table = jnp.concatenate([right_ref[0], right_ref[0], right_ref[1]], 0)
    return dot(jnp.concatenate([high, low, high], 1), table)


def left_stage(first, width, left_ref):
    modes = first.shape[0] // width
    cols = jnp.concatenate(
        [
            jnp.concatenate(
                [first[m * width : (m + 1) * width, part * width : (part + 1) * width] for m in range(modes)], 1
            )
            for part in range(2)
        ],
        0,
    )
    high, low = halves(cols)
    table = jnp.concatenate([left_ref[: 2 * width], left_ref[: 2 * width], left_ref[2 * width :]], 1)
    second = dot(table, jnp.concatenate([high, low, high], 0))
    return [
        (second[:width, m * width : (m + 1) * width], second[width:, m * width : (m + 1) * width])
        for m in range(modes)
    ]


def two_sided(blocks, right_ref, left_ref, group=2):
    width = blocks[0][0].shape[0]
    firsts = [right_stage(blocks[i : i + group], right_ref) for i in range(0, len(blocks), group)]
    return [block for first in firsts for block in left_stage(first, width, left_ref)]


def times(left, right):
    return left[0] * right[0] - left[1] * right[1], left[0] * right[1] + left[1] * right[0]


def window_place(place_ref, slot, slots, width, blocks):
    row_start, col_start = place_ref[slot], place_ref[slots + slot]
    block = col_start // width
    shift = col_start - block * width
    lane = lax.broadcasted_iota(jnp.int32, (width, width), 1)
    row = lax.broadcasted_iota(jnp.int32, (width, width), 0)
    first = pl.ds(pl.multiple_of(block * width, width), width)
    second = pl.ds(pl.multiple_of(jnp.minimum(block + 1, blocks - 1) * width, width), width)
    return row >= row_start, lane >= shift, shift, first, second


def load_kernel(*refs):
    count = len(refs) // 2
    for source, target in zip(refs[:count], refs[count:]):
        target[...] = source[...]


def strip_kernel(start, before_ref, object_ref, strip_ref):
    size, planes, width, _ = strip_ref.shape
    slots = before_ref.shape[0] // 2
    for i in range(size):
        _, in_first, _, first, second = window_place(before_ref, start + i, slots, width, object_ref.shape[-1] // width)
        for plane in range(planes):
            strip_ref[i, plane] = jnp.where(
                in_first, object_ref[plane // 2, plane % 2, :, first], object_ref[plane // 2, plane % 2, :, second]
            )


PAIR = 3
PIECES = ((1, 1), (2, 1), (3, 1))


def gradient_kernel(
    start, axis, counts_ref, place_ref, object_ref, probe_ref, measured_ref, fr_ref, fl_ref, pr_ref, pl_ref, *refs
):
    first_call = start == 0
    tile = lax.axis_index(axis)
    count = counts_ref[tile]
    modes, _, width, _ = probe_ref.shape
    slots = measured_ref.shape[0]
    last_call = start + PAIR == slots
    rim_refs, refs = refs[:PAIR], refs[PAIR:]
    before, refs = (refs[:1], refs[1:]) if not first_call else ((), refs)
    if last_call:
        *grad_refs, kept_ref, sent_ref, sums_ref = refs
    else:
        *grad_refs, sums_ref = refs
    sums_ref[...] = jnp.zeros(sums_ref.shape, F32) if first_call else before[0][...]
    probe = [(probe_ref[m, 0], probe_ref[m, 1]) for m in range(modes)]

    @pl.when(start < count)
    def _():
        places = [
            window_place(place_ref, start + i, slots, width, object_ref.shape[-1] // width) for i in range(PAIR)
        ]

        def window(i, s, part):
            in_own, in_first, shift, first, second = places[i]
            own = jnp.where(in_first, object_ref[s, part, :, first], object_ref[s, part, :, second])
            rim_ref = rim_refs[i]
            stored = jnp.where(in_own, own, rim_ref[(start + i) % rim_ref.shape[0], 2 * s + part])
            stored = pltpu.roll(stored, lax.rem(width - place_ref[start + i], width), 0)
            return pltpu.roll(stored, lax.rem(width - shift, width), 1)

        def put(i, s, part, value):
            value = pltpu.roll(value, place_ref[start + i], 0)
            grad_ref, at = [(ref, at) for ref in grad_refs for at in range(ref.shape[0])][i]
            grad_ref[at, 2 * s + part] = pltpu.roll(value, places[i][2], 1)

        def split(blocks):
            return [blocks[i * modes : (i + 1) * modes] for i in range(PAIR)]

        ones = [(window(i, 0, 0), window(i, 0, 1)) for i in range(PAIR)]
        moved = split(two_sided([times(p, one) for one in ones for p in probe], pr_ref, pl_ref))
        twos = [(window(i, 1, 0), window(i, 1, 1)) for i in range(PAIR)]
        far = split(two_sided([times(w, two) for ws, two in zip(moved, twos) for w in ws], fr_ref, fl_ref))
        back = []
        for i in range(PAIR):
            intensity = sum(re * re + im * im for re, im in far[i])
            residue = 2.0 * (intensity - measured_ref[start + i])
            back += [(residue * re, -(residue * im)) for re, im in far[i]]
        back = split(two_sided(back, fr_ref, fl_ref))
        last = split(two_sided([times(g, two) for gs, two in zip(back, twos) for g in gs], pr_ref, pl_ref))
        for i in range(PAIR):
            terms = [times(w, g) for w, g in zip(moved[i], back[i])]
            put(i, 1, 0, sum(t[0] for t in terms))
            put(i, 1, 1, -sum(t[1] for t in terms))
            terms = [times(p, g) for p, g in zip(probe, last[i])]
            put(i, 0, 0, sum(t[0] for t in terms))
            put(i, 0, 1, -sum(t[1] for t in terms))
        live = [start + i < count for i in range(PAIR)]

        def summed(values):
            return sum(jnp.where(alive, value, 0.0) for alive, value in zip(live, values))

        for m in range(modes):
            grads = [times(one, g[m]) for one, g in zip(ones, last)]
            for part, sign in ((0, 1.0), (1, -1.0)):
                rows = pl.ds((2 * m + part) * width, width)
                sums_ref[rows] += sign * summed(g[part] for g in grads)
        sums_ref[pl.ds(2 * modes * width, width)] += summed(re * re + im * im for re, im in ones)
    if last_call:
        half = kept_ref.shape[0]
        side = lax.rem(tile, 2)
        kept_ref[...] = sums_ref[pl.ds(pl.multiple_of(side * half, 8), half)]
        sent_ref[...] = sums_ref[pl.ds(pl.multiple_of((1 - side) * half, 8), half)]


def add_windows(target_ref, counts_ref, place_ref, before_ref, axis, window_of):
    tile = lax.axis_index(axis)
    width, slots = target_ref.shape[0], place_ref.shape[0] // 2
    target_ref[...] = jnp.zeros(target_ref.shape, F32)
    for slot in range(slots):
        for own in (True, False):
            ref = place_ref if own else before_ref
            count = counts_ref[tile] if own else jnp.where(tile > 0, counts_ref[jnp.maximum(tile - 1, 0)], 0)

            @pl.when(slot < count)
            def _():
                in_own, in_first, shift, first, second = window_place(
                    ref, slot, slots, width, target_ref.shape[1] // width
                )
                value = window_of(ref, slot, own, shift)
                wanted = in_own if own else jnp.logical_not(in_own)
                value = jnp.where(wanted, value, 0.0)
                target_ref[:, first] += jnp.where(in_first, value, 0.0)
                target_ref[:, second] += jnp.where(in_first, 0.0, value)


def light_kernel(axis, counts_ref, place_ref, before_ref, probe_ref, lit_ref):
    modes = probe_ref.shape[0]
    power = sum(probe_ref[m, part] * probe_ref[m, part] for m in range(modes) for part in range(2))

    def window_of(ref, slot, own, shift):
        return pltpu.roll(pltpu.roll(power, ref[slot], 0), shift, 1)

    add_windows(lit_ref, counts_ref, place_ref, before_ref, axis, window_of)
    lit_ref[...] = 0.5 / (lit_ref[...] + 1.0)


def copy_kernel(source_ref, out_ref):
    out_ref[...] = source_ref[...]


def update_kernel(axis, counts_ref, place_ref, before_ref, object_ref, lit_ref, *refs):
    *refs, out_ref, sum_ref = refs
    plane = pl.program_id(0)
    own_refs, rim_refs = refs[: len(refs) // 2], refs[len(refs) // 2 :]

    def window_of(ref, slot, own, shift):
        parts = [(r, i) for r in (own_refs if own else rim_refs) for i in range(r.shape[0])]
        return parts[slot][0][parts[slot][1], plane]

    add_windows(sum_ref, counts_ref, place_ref, before_ref, axis, window_of)
    out_ref[0, 0] = object_ref[plane // 2, plane % 2] - sum_ref[...] * lit_ref[...]


def probe_kernel(axis, mine_ref, got_ref, probe_ref, out_ref, total_ref):
    modes, _, width, _ = probe_ref.shape
    half = mine_ref.shape[0]
    side = lax.rem(lax.axis_index(axis), 2)
    total_ref[pl.ds(pl.multiple_of(side * half, 8), half)] = mine_ref[...]
    total_ref[pl.ds(pl.multiple_of((1 - side) * half, 8), half)] = got_ref[...]
    scale = 0.5 / (total_ref[pl.ds(2 * modes * width, width)] + 1.0)
    for m in range(modes):
        for part in range(2):
            out_ref[m, part] = probe_ref[m, part] - total_ref[pl.ds((2 * m + part) * width, width)] * scale


def after(value, *others):
    return lax.optimization_barrier((value, *others))[0]


def halve_kernel(axis, bit, kept_ref, got_ref, next_kept_ref, next_sent_ref):
    half = next_kept_ref.shape[0]
    side = lax.rem(lax.axis_index(axis) // bit, 2)
    for ref, which in ((next_kept_ref, side), (next_sent_ref, 1 - side)):
        rows = pl.ds(pl.multiple_of(which * half, 8), half)
        ref[...] = kept_ref[rows] + got_ref[rows]


def add_kernel(kept_ref, got_ref, out_ref):
    out_ref[...] = kept_ref[...] + got_ref[...]


def join_kernel(axis, bit, mine_ref, got_ref, out_ref):
    half = mine_ref.shape[0]
    side = lax.rem(lax.axis_index(axis) // bit, 2)
    out_ref[pl.ds(pl.multiple_of(side * half, 8), half)] = mine_ref[...]
    out_ref[pl.ds(pl.multiple_of((1 - side) * half, 8), half)] = got_ref[...]


def half_sum(kept, sent, axis, beside, waits):
    count = lax.axis_size(axis)
    bits = [1 << b for b in range(count.bit_length() - 1)]
    vmem = pl.BlockSpec(memory_space=pltpu.VMEM)
    width = kept.shape[1]

    def exchanged(value, bit, step):
        value = after(value, *waits(step))
        got = lax.ppermute(value, axis, [(i, i ^ bit) for i in range(count)])
        beside(step, value)
        return pltpu.with_memory_space_constraint(got, pltpu.VMEM)

    def local(kernel, rows, *operands):
        return pl.pallas_call(
            kernel,
            out_shape=[pltpu.VMEM((n, width), F32) for n in rows],
            in_specs=[vmem] * 2,
            out_specs=[vmem] * len(rows),
            compiler_params=pltpu.CompilerParams(vmem_limit_bytes=4 << 20),
        )(*operands)

    got = exchanged(sent, bits[0], 0)
    halved = bits[1:3]
    for step, bit in enumerate(bits[1:], 1):
        rows = kept.shape[0]
        if bit in halved:
            kept, sent = local(functools.partial(halve_kernel, axis, bit), (rows // 2,) * 2, kept, got)
        else:
            (kept,) = local(add_kernel, (rows,), kept, got)
            sent = kept
        got = exchanged(sent, bit, step)
    (value,) = local(add_kernel, kept.shape[:1], kept, got)
    for step, bit in enumerate(reversed(halved), len(bits)):
        got = exchanged(value, bit, step)
        (value,) = local(functools.partial(join_kernel, axis, bit), (2 * value.shape[0],), value, got)
    return value, exchanged(value, bits[0], len(bits) + len(halved))


def body(object_field, probe_modes, measured, row_offset, col_offset, tile_counts):
    axis = "tile"
    slices, _, tile_rows, tile_cols = object_field.shape
    modes, _, width, _ = probe_modes.shape
    slots = measured.shape[0]
    dft, move = complex_tables(width)
    smem = pl.BlockSpec(memory_space=pltpu.SMEM)
    vmem = pl.BlockSpec(memory_space=pltpu.VMEM)
    params = pltpu.CompilerParams(vmem_limit_bytes=16 << 20)

    def held(value):
        return pltpu.with_memory_space_constraint(value, pltpu.VMEM)

    place = jnp.concatenate([row_offset, col_offset])
    before = passed_along(place, axis, 1)

    def load(*arrays):
        return pl.pallas_call(
            load_kernel,
            out_shape=tuple(pltpu.VMEM(a.shape, a.dtype) for a in arrays),
            in_specs=[vmem] * len(arrays),
            out_specs=(vmem,) * len(arrays),
            compiler_params=params,
        )(*arrays)

    (objects,) = load(object_field)
    in_chunk = PAIR

    def windows(size):
        return pltpu.VMEM((size, 2 * slices, width, width), F32)

    rims, strip = [], before
    for start in range(0, slots, in_chunk):
        strip = pl.pallas_call(
            functools.partial(strip_kernel, start),
            out_shape=windows(in_chunk),
            in_specs=[smem, vmem],
            out_specs=vmem,
            compiler_params=params,
        )(after(before, strip), objects)
        rims.append(held(passed_along(strip, axis, -1)))
    tables = [jnp.asarray(t) for t in (*real_forms(dft), *real_forms(move))]
    probe, patterns, *tables = load(*lax.optimization_barrier((strip, probe_modes, measured, *tables))[1:])
    lit = pl.pallas_call(
        functools.partial(light_kernel, axis),
        out_shape=pltpu.VMEM((tile_rows, tile_cols), F32),
        in_specs=[smem, smem, smem, vmem],
        out_specs=vmem,
        compiler_params=params,
    )(tile_counts, place, after(before, strip), probe)
    rows = (2 * modes + 1) * width
    whole, half = pltpu.VMEM((rows, width), F32), pltpu.VMEM((rows // 2, width), F32)
    common = (probe, patterns, *tables)
    grads, arrived, sums = [], [], []
    for start in range(0, slots, PAIR):
        last_call = start + PAIR == slots
        ready = arrived[: start // PAIR - 1] if start else [lit]
        pieces = [windows(size) for _, size in PIECES] if last_call else [windows(PAIR)]
        results = pieces + ([half, half] if last_call else [whole])
        outs = pl.pallas_call(
            functools.partial(gradient_kernel, start, axis),
            out_shape=results,
            in_specs=[smem] * 2 + [vmem] * (7 + PAIR + len(sums)),
            out_specs=[vmem] * len(results),
            scratch_shapes=[whole] if last_call else [],
            compiler_params=params,
            cost_estimate=pl.CostEstimate(flops=1, bytes_accessed=6 << 20, transcendentals=0),
        )(
            tile_counts, after(place, *ready), objects, *common,
            *(rims[(start + i) // in_chunk] for i in range(PAIR)), *sums,
        )
        grads += outs[: len(pieces)]
        sums = outs[len(pieces) :]
        if not last_call:
            arrived.append(passed_along(outs[0], axis, 1))

    def beside(step, value):
        for n, (when, size) in enumerate(PIECES):
            if when == step:
                piece = pl.pallas_call(
                    copy_kernel,
                    out_shape=windows(size),
                    in_specs=[vmem],
                    out_specs=vmem,
                    compiler_params=params,
                    cost_estimate=pl.CostEstimate(flops=1, bytes_accessed=6 << 20, transcendentals=0),
                )(after(grads[n - len(PIECES)], value))
                arrived.append(passed_along(piece, axis, 1))

    updated = []

    def waits(step):
        if step == 1:
            return arrived
        last = lax.axis_size(axis).bit_length() - 1 + 2
        if step == last - 1:
            return arrived
        if step == last:
            updated.append(update())
            return updated
        return []

    def update():
        return pl.pallas_call(
            functools.partial(update_kernel, axis),
            grid=(2 * slices,),
            out_shape=jax.ShapeDtypeStruct(object_field.shape, F32),
            in_specs=[smem] * 3 + [vmem] * (2 + 2 * len(grads)),
            out_specs=pl.BlockSpec((1, 1, tile_rows, tile_cols), lambda plane: (plane // 2, plane % 2, 0, 0)),
            scratch_shapes=[pltpu.VMEM((tile_rows, tile_cols), F32)],
            compiler_params=params,
            cost_estimate=pl.CostEstimate(flops=1, bytes_accessed=12 << 20, transcendentals=0),
        )(tile_counts, place, before, objects, lit, *grads, *map(held, arrived))

    mine, got = half_sum(*sums, axis, beside, waits)
    updated_probe = pl.pallas_call(
        functools.partial(probe_kernel, axis),
        out_shape=jax.ShapeDtypeStruct(probe_modes.shape, F32),
        in_specs=[vmem] * 3,
        out_specs=vmem,
        scratch_shapes=[pltpu.VMEM((rows, width), F32)],
        compiler_params=params,
    )(mine, got, probe)
    return (updated[0], updated_probe)


def solution(mesh):
    return jax.shard_map(
        body,
        mesh=mesh,
        in_specs=(
            P("groups", None, "tile", None),
            P("groups", None, None, None),
            P(("groups", "tile"), None, None),
            P(("groups", "tile")),
            P(("groups", "tile")),
            P("groups"),
        ),
        out_specs=(P("groups", None, "tile", None), P("groups", None, None, None)),
        check_vma=False,
    )
```

```python
import functools
import math

import jax
import jax.numpy as jnp
import ml_dtypes
import numpy as np
from jax import lax
from jax.experimental import pallas as pl
from jax.experimental.pallas import tpu as pltpu
from jax.sharding import PartitionSpec as P

F32, BF16 = jnp.float32, jnp.bfloat16


def passed_along(value, axis, steps):
    count = lax.axis_size(axis)
    leading, last = (max(0, -steps), min(count, count - steps))
    return lax.ppermute(value, axis, [(source, source + steps) for source in range(leading, last)])


def complex_tables(width):
    index = np.arange(width)
    angle = 2.0 * math.pi / width * (index[:, None] * index[None, :] % width)
    dft = np.exp(-1j * angle) / math.sqrt(width)
    frequency = np.where(index < width // 2, index, index - width).astype(np.float64)
    phase = np.exp(-0.5j * math.pi / width * frequency**2)
    return dft, np.conj(dft) @ (phase[:, None] * dft)


def real_forms(table):
    re, im = table.real, table.imag
    right = np.block([[re, im], [-im, re]])
    left = np.block([[re, -im], [im, re]])

    def parts(matrix):
        high = matrix.astype(ml_dtypes.bfloat16)
        low = (matrix - high.astype(np.float64)).astype(ml_dtypes.bfloat16)
        return high, low

    right_high, right_low = parts(right)
    left_high, left_low = parts(left)
    return np.stack([right_high, right_low]), np.concatenate([left_high, left_low], 0)


def halves(value):
    high = value.astype(BF16)
    return high, (value - high.astype(F32)).astype(BF16)


def dot(left, right):
    return jnp.dot(left, right, preferred_element_type=F32)


def right_stage(blocks, right_ref):
    rows = jnp.concatenate([jnp.concatenate(pair, 1) for pair in blocks], 0)
    high, low = halves(rows)
    table = jnp.concatenate([right_ref[0], right_ref[0], right_ref[1]], 0)
    return dot(jnp.concatenate([high, low, high], 1), table)


def left_stage(first, width, left_ref):
    modes = first.shape[0] // width
    cols = jnp.concatenate(
        [
            jnp.concatenate(
                [first[m * width : (m + 1) * width, part * width : (part + 1) * width] for m in range(modes)], 1
            )
            for part in range(2)
        ],
        0,
    )
    high, low = halves(cols)
    table = jnp.concatenate([left_ref[: 2 * width], left_ref[: 2 * width], left_ref[2 * width :]], 1)
    second = dot(table, jnp.concatenate([high, low, high], 0))
    return [
        (second[:width, m * width : (m + 1) * width], second[width:, m * width : (m + 1) * width])
        for m in range(modes)
    ]


def two_sided(blocks, right_ref, left_ref, group=2):
    width = blocks[0][0].shape[0]
    firsts = [right_stage(blocks[i : i + group], right_ref) for i in range(0, len(blocks), group)]
    return [block for first in firsts for block in left_stage(first, width, left_ref)]


def times(left, right):
    return left[0] * right[0] - left[1] * right[1], left[0] * right[1] + left[1] * right[0]


def window_place(place_ref, slot, slots, width, blocks):
    row_start, col_start = place_ref[slot], place_ref[slots + slot]
    block = col_start // width
    shift = col_start - block * width
    lane = lax.broadcasted_iota(jnp.int32, (width, width), 1)
    row = lax.broadcasted_iota(jnp.int32, (width, width), 0)
    first = pl.ds(pl.multiple_of(block * width, width), width)
    second = pl.ds(pl.multiple_of(jnp.minimum(block + 1, blocks - 1) * width, width), width)
    return row >= row_start, lane >= shift, shift, first, second


def load_kernel(*refs):
    count = len(refs) // 2
    for source, target in zip(refs[:count], refs[count:]):
        target[...] = source[...]


def strip_kernel(start, before_ref, object_ref, strip_ref):
    size, planes, width, _ = strip_ref.shape
    slots = before_ref.shape[0] // 2
    for i in range(size):
        _, in_first, _, first, second = window_place(before_ref, start + i, slots, width, object_ref.shape[-1] // width)
        for plane in range(planes):
            strip_ref[i, plane] = jnp.where(
                in_first, object_ref[plane // 2, plane % 2, :, first], object_ref[plane // 2, plane % 2, :, second]
            )


PAIR = 3
PIECES = ((0, 1), (1, 1), (2, 1))


def gradient_kernel(
    start, axis, counts_ref, place_ref, object_ref, probe_ref, measured_ref, fr_ref, fl_ref, pr_ref, pl_ref, *refs
):
    first_call = start == 0
    tile = lax.axis_index(axis)
    count = counts_ref[tile]
    modes, _, width, _ = probe_ref.shape
    slots = measured_ref.shape[0]
    last_call = start + PAIR == slots
    rim_refs, refs = refs[:PAIR], refs[PAIR:]
    before, refs = (refs[:1], refs[1:]) if not first_call else ((), refs)
    if last_call:
        *grad_refs, kept_ref, sent_ref, sums_ref = refs
    else:
        *grad_refs, sums_ref = refs
    sums_ref[...] = jnp.zeros(sums_ref.shape, F32) if first_call else before[0][...]
    probe = [(probe_ref[m, 0], probe_ref[m, 1]) for m in range(modes)]

    @pl.when(start < count)
    def _():
        places = [
            window_place(place_ref, start + i, slots, width, object_ref.shape[-1] // width) for i in range(PAIR)
        ]

        def window(i, s, part):
            in_own, in_first, shift, first, second = places[i]
            own = jnp.where(in_first, object_ref[s, part, :, first], object_ref[s, part, :, second])
            rim_ref = rim_refs[i]
            stored = jnp.where(in_own, own, rim_ref[(start + i) % rim_ref.shape[0], 2 * s + part])
            stored = pltpu.roll(stored, lax.rem(width - place_ref[start + i], width), 0)
            return pltpu.roll(stored, lax.rem(width - shift, width), 1)

        def put(i, s, part, value):
            value = pltpu.roll(value, place_ref[start + i], 0)
            grad_ref, at = [(ref, at) for ref in grad_refs for at in range(ref.shape[0])][i]
            grad_ref[at, 2 * s + part] = pltpu.roll(value, places[i][2], 1)

        def split(blocks):
            return [blocks[i * modes : (i + 1) * modes] for i in range(PAIR)]

        ones = [(window(i, 0, 0), window(i, 0, 1)) for i in range(PAIR)]
        moved = split(two_sided([times(p, one) for one in ones for p in probe], pr_ref, pl_ref))
        twos = [(window(i, 1, 0), window(i, 1, 1)) for i in range(PAIR)]
        far = split(two_sided([times(w, two) for ws, two in zip(moved, twos) for w in ws], fr_ref, fl_ref))
        back = []
        for i in range(PAIR):
            intensity = sum(re * re + im * im for re, im in far[i])
            residue = 2.0 * (intensity - measured_ref[start + i])
            back += [(residue * re, -(residue * im)) for re, im in far[i]]
        back = split(two_sided(back, fr_ref, fl_ref))
        last = split(two_sided([times(g, two) for gs, two in zip(back, twos) for g in gs], pr_ref, pl_ref))
        for i in range(PAIR):
            terms = [times(w, g) for w, g in zip(moved[i], back[i])]
            put(i, 1, 0, sum(t[0] for t in terms))
            put(i, 1, 1, -sum(t[1] for t in terms))
            terms = [times(p, g) for p, g in zip(probe, last[i])]
            put(i, 0, 0, sum(t[0] for t in terms))
            put(i, 0, 1, -sum(t[1] for t in terms))
        live = [start + i < count for i in range(PAIR)]

        def summed(values):
            return sum(jnp.where(alive, value, 0.0) for alive, value in zip(live, values))

        for m in range(modes):
            grads = [times(one, g[m]) for one, g in zip(ones, last)]
            for part, sign in ((0, 1.0), (1, -1.0)):
                rows = pl.ds((2 * m + part) * width, width)
                sums_ref[rows] += sign * summed(g[part] for g in grads)
        sums_ref[pl.ds(2 * modes * width, width)] += summed(re * re + im * im for re, im in ones)
    if last_call:
        half = kept_ref.shape[0]
        side = lax.rem(tile, 2)
        kept_ref[...] = sums_ref[pl.ds(pl.multiple_of(side * half, 8), half)]
        sent_ref[...] = sums_ref[pl.ds(pl.multiple_of((1 - side) * half, 8), half)]


def add_windows(target_ref, counts_ref, place_ref, before_ref, axis, window_of):
    tile = lax.axis_index(axis)
    width, slots = target_ref.shape[0], place_ref.shape[0] // 2
    target_ref[...] = jnp.zeros(target_ref.shape, F32)
    for slot in range(slots):
        for own in (True, False):
            ref = place_ref if own else before_ref
            count = counts_ref[tile] if own else jnp.where(tile > 0, counts_ref[jnp.maximum(tile - 1, 0)], 0)

            @pl.when(slot < count)
            def _():
                in_own, in_first, shift, first, second = window_place(
                    ref, slot, slots, width, target_ref.shape[1] // width
                )
                value = window_of(ref, slot, own, shift)
                wanted = in_own if own else jnp.logical_not(in_own)
                value = jnp.where(wanted, value, 0.0)
                target_ref[:, first] += jnp.where(in_first, value, 0.0)
                target_ref[:, second] += jnp.where(in_first, 0.0, value)


def light_kernel(axis, counts_ref, place_ref, before_ref, probe_ref, lit_ref):
    modes = probe_ref.shape[0]
    power = sum(probe_ref[m, part] * probe_ref[m, part] for m in range(modes) for part in range(2))

    def window_of(ref, slot, own, shift):
        return pltpu.roll(pltpu.roll(power, ref[slot], 0), shift, 1)

    add_windows(lit_ref, counts_ref, place_ref, before_ref, axis, window_of)
    lit_ref[...] = 0.5 / (lit_ref[...] + 1.0)


def copy_kernel(source_ref, out_ref):
    out_ref[...] = source_ref[...]


def update_kernel(axis, counts_ref, place_ref, before_ref, object_ref, lit_ref, *refs):
    *refs, out_ref, sum_ref = refs
    plane = pl.program_id(0)
    own_refs, rim_refs = refs[: len(refs) // 2], refs[len(refs) // 2 :]

    def window_of(ref, slot, own, shift):
        parts = [(r, i) for r in (own_refs if own else rim_refs) for i in range(r.shape[0])]
        return parts[slot][0][parts[slot][1], plane]

    add_windows(sum_ref, counts_ref, place_ref, before_ref, axis, window_of)
    out_ref[0, 0] = object_ref[plane // 2, plane % 2] - sum_ref[...] * lit_ref[...]


def probe_kernel(axis, mine_ref, got_ref, probe_ref, out_ref, total_ref):
    modes, _, width, _ = probe_ref.shape
    half = mine_ref.shape[0]
    side = lax.rem(lax.axis_index(axis), 2)
    total_ref[pl.ds(pl.multiple_of(side * half, 8), half)] = mine_ref[...]
    total_ref[pl.ds(pl.multiple_of((1 - side) * half, 8), half)] = got_ref[...]
    scale = 0.5 / (total_ref[pl.ds(2 * modes * width, width)] + 1.0)
    for m in range(modes):
        for part in range(2):
            out_ref[m, part] = probe_ref[m, part] - total_ref[pl.ds((2 * m + part) * width, width)] * scale


def after(value, *others):
    return lax.optimization_barrier((value, *others))[0]


def halve_kernel(axis, bit, kept_ref, got_ref, next_kept_ref, next_sent_ref):
    half = next_kept_ref.shape[0]
    side = lax.rem(lax.axis_index(axis) // bit, 2)
    for ref, which in ((next_kept_ref, side), (next_sent_ref, 1 - side)):
        rows = pl.ds(pl.multiple_of(which * half, 8), half)
        ref[...] = kept_ref[rows] + got_ref[rows]


def add_kernel(kept_ref, got_ref, out_ref):
    out_ref[...] = kept_ref[...] + got_ref[...]


def join_kernel(axis, bit, mine_ref, got_ref, out_ref):
    half = mine_ref.shape[0]
    side = lax.rem(lax.axis_index(axis) // bit, 2)
    out_ref[pl.ds(pl.multiple_of(side * half, 8), half)] = mine_ref[...]
    out_ref[pl.ds(pl.multiple_of((1 - side) * half, 8), half)] = got_ref[...]


def half_sum(kept, sent, axis, beside, waits):
    count = lax.axis_size(axis)
    bits = [1 << b for b in range(count.bit_length() - 1)]
    bits = bits[:1] + bits[2:] + bits[1:2]
    vmem = pl.BlockSpec(memory_space=pltpu.VMEM)
    width = kept.shape[1]

    def exchanged(value, bit, step):
        value = after(value, *waits(step))
        got = lax.ppermute(value, axis, [(i, i ^ bit) for i in range(count)])
        beside(step, value)
        return pltpu.with_memory_space_constraint(got, pltpu.VMEM)

    def local(kernel, rows, *operands):
        return pl.pallas_call(
            kernel,
            out_shape=[pltpu.VMEM((n, width), F32) for n in rows],
            in_specs=[vmem] * 2,
            out_specs=[vmem] * len(rows),
            compiler_params=pltpu.CompilerParams(vmem_limit_bytes=4 << 20),
        )(*operands)

    got = exchanged(sent, bits[0], 0)
    halved = bits[1:3]
    for step, bit in enumerate(bits[1:], 1):
        rows = kept.shape[0]
        if bit in halved:
            kept, sent = local(functools.partial(halve_kernel, axis, bit), (rows // 2,) * 2, kept, got)
        else:
            (kept,) = local(add_kernel, (rows,), kept, got)
            sent = kept
        got = exchanged(sent, bit, step)
    (value,) = local(add_kernel, kept.shape[:1], kept, got)
    for step, bit in enumerate(reversed(halved), len(bits)):
        got = exchanged(value, bit, step)
        (value,) = local(functools.partial(join_kernel, axis, bit), (2 * value.shape[0],), value, got)
    return value, exchanged(value, bits[0], len(bits) + len(halved))


def body(object_field, probe_modes, measured, row_offset, col_offset, tile_counts):
    axis = "tile"
    slices, _, tile_rows, tile_cols = object_field.shape
    modes, _, width, _ = probe_modes.shape
    slots = measured.shape[0]
    dft, move = complex_tables(width)
    smem = pl.BlockSpec(memory_space=pltpu.SMEM)
    vmem = pl.BlockSpec(memory_space=pltpu.VMEM)
    params = pltpu.CompilerParams(vmem_limit_bytes=16 << 20)

    def held(value):
        return pltpu.with_memory_space_constraint(value, pltpu.VMEM)

    place = jnp.concatenate([row_offset, col_offset])
    before = passed_along(place, axis, 1)

    def load(*arrays):
        return pl.pallas_call(
            load_kernel,
            out_shape=tuple(pltpu.VMEM(a.shape, a.dtype) for a in arrays),
            in_specs=[vmem] * len(arrays),
            out_specs=(vmem,) * len(arrays),
            compiler_params=params,
        )(*arrays)

    (objects,) = load(object_field)
    in_chunk = PAIR

    def windows(size):
        return pltpu.VMEM((size, 2 * slices, width, width), F32)

    rims, strip = [], before
    for start in range(0, slots, in_chunk):
        strip = pl.pallas_call(
            functools.partial(strip_kernel, start),
            out_shape=windows(in_chunk),
            in_specs=[smem, vmem],
            out_specs=vmem,
            compiler_params=params,
        )(after(before, strip), objects)
        rims.append(held(passed_along(strip, axis, -1)))
    tables = [jnp.asarray(t) for t in (*real_forms(dft), *real_forms(move))]
    probe, patterns, *tables = load(*lax.optimization_barrier((strip, probe_modes, measured, *tables))[1:])
    lit = pl.pallas_call(
        functools.partial(light_kernel, axis),
        out_shape=pltpu.VMEM((tile_rows, tile_cols), F32),
        in_specs=[smem, smem, smem, vmem],
        out_specs=vmem,
        compiler_params=params,
    )(tile_counts, place, after(before, strip), probe)
    rows = (2 * modes + 1) * width
    whole, half = pltpu.VMEM((rows, width), F32), pltpu.VMEM((rows // 2, width), F32)
    common = (probe, patterns, *tables)
    grads, arrived, sums = [], [], []
    for start in range(0, slots, PAIR):
        last_call = start + PAIR == slots
        ready = arrived[: start // PAIR - 1] if start else [lit]
        pieces = [windows(size) for _, size in PIECES] if last_call else [windows(PAIR)]
        results = pieces + ([half, half] if last_call else [whole])
        outs = pl.pallas_call(
            functools.partial(gradient_kernel, start, axis),
            out_shape=results,
            in_specs=[smem] * 2 + [vmem] * (7 + PAIR + len(sums)),
            out_specs=[vmem] * len(results),
            scratch_shapes=[whole] if last_call else [],
            compiler_params=params,
            cost_estimate=pl.CostEstimate(flops=1, bytes_accessed=6 << 20, transcendentals=0),
        )(
            tile_counts, after(place, *ready), objects, *common,
            *(rims[(start + i) // in_chunk] for i in range(PAIR)), *sums,
        )
        grads += outs[: len(pieces)]
        sums = outs[len(pieces) :]
        if not last_call:
            arrived.append(passed_along(outs[0], axis, 1))

    def beside(step, value):
        for n, (when, size) in enumerate(PIECES):
            if when == step:
                piece = pl.pallas_call(
                    copy_kernel,
                    out_shape=windows(size),
                    in_specs=[vmem],
                    out_specs=vmem,
                    compiler_params=params,
                    cost_estimate=pl.CostEstimate(flops=1, bytes_accessed=6 << 20, transcendentals=0),
                )(after(grads[n - len(PIECES)], value))
                arrived.append(passed_along(piece, axis, 1))

    updated = []

    def waits(step):
        if step == 3:
            return arrived[: (1 if step == 3 else 9)]
        last = lax.axis_size(axis).bit_length() - 1 + 2
        if step == last - 1:
            return arrived[: (1 if step == 3 else 9)]
        if step == last:
            updated.append(update())
            return updated
        return []

    def update():
        return pl.pallas_call(
            functools.partial(update_kernel, axis),
            grid=(2 * slices,),
            out_shape=jax.ShapeDtypeStruct(object_field.shape, F32),
            in_specs=[smem] * 3 + [vmem] * (2 + 2 * len(grads)),
            out_specs=pl.BlockSpec((1, 1, tile_rows, tile_cols), lambda plane: (plane // 2, plane % 2, 0, 0)),
            scratch_shapes=[pltpu.VMEM((tile_rows, tile_cols), F32)],
            compiler_params=params,
            cost_estimate=pl.CostEstimate(flops=1, bytes_accessed=12 << 20, transcendentals=0),
        )(tile_counts, place, before, objects, lit, *grads, *map(held, arrived))

    mine, got = half_sum(*sums, axis, beside, waits)
    updated_probe = pl.pallas_call(
        functools.partial(probe_kernel, axis),
        out_shape=jax.ShapeDtypeStruct(probe_modes.shape, F32),
        in_specs=[vmem] * 3,
        out_specs=vmem,
        scratch_shapes=[pltpu.VMEM((rows, width), F32)],
        compiler_params=params,
    )(mine, got, probe)
    return (updated[0], updated_probe)


def solution(mesh):
    return jax.shard_map(
        body,
        mesh=mesh,
        in_specs=(
            P("groups", None, "tile", None),
            P("groups", None, None, None),
            P(("groups", "tile"), None, None),
            P(("groups", "tile")),
            P(("groups", "tile")),
            P("groups"),
        ),
        out_specs=(P("groups", None, "tile", None), P("groups", None, None, None)),
        check_vma=False,
    )
```

```python
import functools
import math

import jax
import jax.numpy as jnp
import ml_dtypes
import numpy as np
from jax import lax
from jax.experimental import pallas as pl
from jax.experimental.pallas import tpu as pltpu
from jax.sharding import PartitionSpec as P

F32, BF16 = jnp.float32, jnp.bfloat16


def passed_along(value, axis, steps):
    count = lax.axis_size(axis)
    leading, last = (max(0, -steps), min(count, count - steps))
    return lax.ppermute(value, axis, [(source, source + steps) for source in range(leading, last)])


def complex_tables(width):
    index = np.arange(width)
    angle = 2.0 * math.pi / width * (index[:, None] * index[None, :] % width)
    dft = np.exp(-1j * angle) / math.sqrt(width)
    frequency = np.where(index < width // 2, index, index - width).astype(np.float64)
    phase = np.exp(-0.5j * math.pi / width * frequency**2)
    return dft, np.conj(dft) @ (phase[:, None] * dft)


def real_forms(table):
    re, im = table.real, table.imag
    right = np.block([[re, im], [-im, re]])
    left = np.block([[re, -im], [im, re]])

    def parts(matrix):
        high = matrix.astype(ml_dtypes.bfloat16)
        low = (matrix - high.astype(np.float64)).astype(ml_dtypes.bfloat16)
        return high, low

    right_high, right_low = parts(right)
    left_high, left_low = parts(left)
    return np.stack([right_high, right_low]), np.concatenate([left_high, left_low], 0)


def halves(value):
    high = value.astype(BF16)
    return high, (value - high.astype(F32)).astype(BF16)


def dot(left, right):
    return jnp.dot(left, right, preferred_element_type=F32)


def right_stage(blocks, right_ref):
    rows = jnp.concatenate([jnp.concatenate(pair, 1) for pair in blocks], 0)
    high, low = halves(rows)
    table = jnp.concatenate([right_ref[0], right_ref[0], right_ref[1]], 0)
    return dot(jnp.concatenate([high, low, high], 1), table)


def left_stage(first, width, left_ref):
    modes = first.shape[0] // width
    cols = jnp.concatenate(
        [
            jnp.concatenate(
                [first[m * width : (m + 1) * width, part * width : (part + 1) * width] for m in range(modes)], 1
            )
            for part in range(2)
        ],
        0,
    )
    high, low = halves(cols)
    table = jnp.concatenate([left_ref[: 2 * width], left_ref[: 2 * width], left_ref[2 * width :]], 1)
    second = dot(table, jnp.concatenate([high, low, high], 0))
    return [
        (second[:width, m * width : (m + 1) * width], second[width:, m * width : (m + 1) * width])
        for m in range(modes)
    ]


def two_sided(blocks, right_ref, left_ref, group=4):
    width = blocks[0][0].shape[0]
    firsts = [right_stage(blocks[i : i + group], right_ref) for i in range(0, len(blocks), group)]
    return [block for first in firsts for block in left_stage(first, width, left_ref)]


def times(left, right):
    return left[0] * right[0] - left[1] * right[1], left[0] * right[1] + left[1] * right[0]


def window_place(place_ref, slot, slots, width, blocks):
    row_start, col_start = place_ref[slot], place_ref[slots + slot]
    block = col_start // width
    shift = col_start - block * width
    lane = lax.broadcasted_iota(jnp.int32, (width, width), 1)
    row = lax.broadcasted_iota(jnp.int32, (width, width), 0)
    first = pl.ds(pl.multiple_of(block * width, width), width)
    second = pl.ds(pl.multiple_of(jnp.minimum(block + 1, blocks - 1) * width, width), width)
    return row >= row_start, lane >= shift, shift, first, second


def load_kernel(*refs):
    count = len(refs) // 2
    for source, target in zip(refs[:count], refs[count:]):
        target[...] = source[...]


def strip_kernel(start, before_ref, object_ref, strip_ref):
    size, planes, width, _ = strip_ref.shape
    slots = before_ref.shape[0] // 2
    for i in range(size):
        _, in_first, _, first, second = window_place(before_ref, start + i, slots, width, object_ref.shape[-1] // width)
        for plane in range(planes):
            strip_ref[i, plane] = jnp.where(
                in_first, object_ref[plane // 2, plane % 2, :, first], object_ref[plane // 2, plane % 2, :, second]
            )


PAIR = 3
PIECES = ((1, 1), (2, 1), (3, 1))


def gradient_kernel(
    start, axis, counts_ref, place_ref, object_ref, probe_ref, measured_ref, fr_ref, fl_ref, pr_ref, pl_ref, *refs
):
    first_call = start == 0
    tile = lax.axis_index(axis)
    count = counts_ref[tile]
    modes, _, width, _ = probe_ref.shape
    slots = measured_ref.shape[0]
    last_call = start + PAIR == slots
    rim_refs, refs = refs[:PAIR], refs[PAIR:]
    before, refs = (refs[:1], refs[1:]) if not first_call else ((), refs)
    if last_call:
        *grad_refs, kept_ref, sent_ref, sums_ref = refs
    else:
        *grad_refs, sums_ref = refs
    sums_ref[...] = jnp.zeros(sums_ref.shape, F32) if first_call else before[0][...]
    probe = [(probe_ref[m, 0], probe_ref[m, 1]) for m in range(modes)]

    @pl.when(start < count)
    def _():
        places = [
            window_place(place_ref, start + i, slots, width, object_ref.shape[-1] // width) for i in range(PAIR)
        ]

        def window(i, s, part):
            in_own, in_first, shift, first, second = places[i]
            own = jnp.where(in_first, object_ref[s, part, :, first], object_ref[s, part, :, second])
            rim_ref = rim_refs[i]
            stored = jnp.where(in_own, own, rim_ref[(start + i) % rim_ref.shape[0], 2 * s + part])
            stored = pltpu.roll(stored, lax.rem(width - place_ref[start + i], width), 0)
            return pltpu.roll(stored, lax.rem(width - shift, width), 1)

        def put(i, s, part, value):
            value = pltpu.roll(value, place_ref[start + i], 0)
            grad_ref, at = [(ref, at) for ref in grad_refs for at in range(ref.shape[0])][i]
            grad_ref[at, 2 * s + part] = pltpu.roll(value, places[i][2], 1)

        def split(blocks):
            return [blocks[i * modes : (i + 1) * modes] for i in range(PAIR)]

        ones = [(window(i, 0, 0), window(i, 0, 1)) for i in range(PAIR)]
        moved = split(two_sided([times(p, one) for one in ones for p in probe], pr_ref, pl_ref))
        twos = [(window(i, 1, 0), window(i, 1, 1)) for i in range(PAIR)]
        far = split(two_sided([times(w, two) for ws, two in zip(moved, twos) for w in ws], fr_ref, fl_ref))
        back = []
        for i in range(PAIR):
            intensity = sum(re * re + im * im for re, im in far[i])
            residue = 2.0 * (intensity - measured_ref[start + i])
            back += [(residue * re, -(residue * im)) for re, im in far[i]]
        back = split(two_sided(back, fr_ref, fl_ref))
        last = split(two_sided([times(g, two) for gs, two in zip(back, twos) for g in gs], pr_ref, pl_ref))
        for i in range(PAIR):
            terms = [times(w, g) for w, g in zip(moved[i], back[i])]
            put(i, 1, 0, sum(t[0] for t in terms))
            put(i, 1, 1, -sum(t[1] for t in terms))
            terms = [times(p, g) for p, g in zip(probe, last[i])]
            put(i, 0, 0, sum(t[0] for t in terms))
            put(i, 0, 1, -sum(t[1] for t in terms))
        live = [start + i < count for i in range(PAIR)]

        def summed(values):
            return sum(jnp.where(alive, value, 0.0) for alive, value in zip(live, values))

        for m in range(modes):
            grads = [times(one, g[m]) for one, g in zip(ones, last)]
            for part, sign in ((0, 1.0), (1, -1.0)):
                rows = pl.ds((2 * m + part) * width, width)
                sums_ref[rows] += sign * summed(g[part] for g in grads)
        sums_ref[pl.ds(2 * modes * width, width)] += summed(re * re + im * im for re, im in ones)
    if last_call:
        half = kept_ref.shape[0]
        side = lax.rem(tile, 2)
        kept_ref[...] = sums_ref[pl.ds(pl.multiple_of(side * half, 8), half)]
        sent_ref[...] = sums_ref[pl.ds(pl.multiple_of((1 - side) * half, 8), half)]


def add_windows(target_ref, counts_ref, place_ref, before_ref, axis, window_of):
    tile = lax.axis_index(axis)
    width, slots = target_ref.shape[0], place_ref.shape[0] // 2
    target_ref[...] = jnp.zeros(target_ref.shape, F32)
    for slot in range(slots):
        for own in (True, False):
            ref = place_ref if own else before_ref
            count = counts_ref[tile] if own else jnp.where(tile > 0, counts_ref[jnp.maximum(tile - 1, 0)], 0)

            @pl.when(slot < count)
            def _():
                in_own, in_first, shift, first, second = window_place(
                    ref, slot, slots, width, target_ref.shape[1] // width
                )
                value = window_of(ref, slot, own, shift)
                wanted = in_own if own else jnp.logical_not(in_own)
                value = jnp.where(wanted, value, 0.0)
                target_ref[:, first] += jnp.where(in_first, value, 0.0)
                target_ref[:, second] += jnp.where(in_first, 0.0, value)


def light_kernel(axis, counts_ref, place_ref, before_ref, probe_ref, lit_ref):
    modes = probe_ref.shape[0]
    power = sum(probe_ref[m, part] * probe_ref[m, part] for m in range(modes) for part in range(2))

    def window_of(ref, slot, own, shift):
        return pltpu.roll(pltpu.roll(power, ref[slot], 0), shift, 1)

    add_windows(lit_ref, counts_ref, place_ref, before_ref, axis, window_of)
    lit_ref[...] = 0.5 / (lit_ref[...] + 1.0)


def copy_kernel(source_ref, out_ref):
    out_ref[...] = source_ref[...]


def update_kernel(axis, counts_ref, place_ref, before_ref, object_ref, lit_ref, *refs):
    *refs, out_ref, sum_ref = refs
    plane = pl.program_id(0)
    own_refs, rim_refs = refs[: len(refs) // 2], refs[len(refs) // 2 :]

    def window_of(ref, slot, own, shift):
        parts = [(r, i) for r in (own_refs if own else rim_refs) for i in range(r.shape[0])]
        return parts[slot][0][parts[slot][1], plane]

    add_windows(sum_ref, counts_ref, place_ref, before_ref, axis, window_of)
    out_ref[0, 0] = object_ref[plane // 2, plane % 2] - sum_ref[...] * lit_ref[...]


def probe_kernel(axis, mine_ref, got_ref, probe_ref, out_ref, total_ref):
    modes, _, width, _ = probe_ref.shape
    half = mine_ref.shape[0]
    side = lax.rem(lax.axis_index(axis), 2)
    total_ref[pl.ds(pl.multiple_of(side * half, 8), half)] = mine_ref[...]
    total_ref[pl.ds(pl.multiple_of((1 - side) * half, 8), half)] = got_ref[...]
    scale = 0.5 / (total_ref[pl.ds(2 * modes * width, width)] + 1.0)
    for m in range(modes):
        for part in range(2):
            out_ref[m, part] = probe_ref[m, part] - total_ref[pl.ds((2 * m + part) * width, width)] * scale


def after(value, *others):
    return lax.optimization_barrier((value, *others))[0]


def halve_kernel(axis, bit, kept_ref, got_ref, next_kept_ref, next_sent_ref):
    half = next_kept_ref.shape[0]
    side = lax.rem(lax.axis_index(axis) // bit, 2)
    for ref, which in ((next_kept_ref, side), (next_sent_ref, 1 - side)):
        rows = pl.ds(pl.multiple_of(which * half, 8), half)
        ref[...] = kept_ref[rows] + got_ref[rows]


def add_kernel(kept_ref, got_ref, out_ref):
    out_ref[...] = kept_ref[...] + got_ref[...]


def join_kernel(axis, bit, mine_ref, got_ref, out_ref):
    half = mine_ref.shape[0]
    side = lax.rem(lax.axis_index(axis) // bit, 2)
    out_ref[pl.ds(pl.multiple_of(side * half, 8), half)] = mine_ref[...]
    out_ref[pl.ds(pl.multiple_of((1 - side) * half, 8), half)] = got_ref[...]


def half_sum(kept, sent, axis, beside, waits):
    count = lax.axis_size(axis)
    bits = [1 << b for b in range(count.bit_length() - 1)]
    bits = bits[:1] + bits[2:3] + bits[1:2] + bits[3:]
    vmem = pl.BlockSpec(memory_space=pltpu.VMEM)
    width = kept.shape[1]

    def exchanged(value, bit, step):
        value = after(value, *waits(step))
        got = lax.ppermute(value, axis, [(i, i ^ bit) for i in range(count)])
        beside(step, value)
        return pltpu.with_memory_space_constraint(got, pltpu.VMEM)

    def local(kernel, rows, *operands):
        return pl.pallas_call(
            kernel,
            out_shape=[pltpu.VMEM((n, width), F32) for n in rows],
            in_specs=[vmem] * 2,
            out_specs=[vmem] * len(rows),
            compiler_params=pltpu.CompilerParams(vmem_limit_bytes=4 << 20),
        )(*operands)

    got = exchanged(sent, bits[0], 0)
    halved = bits[1:3]
    for step, bit in enumerate(bits[1:], 1):
        rows = kept.shape[0]
        if bit in halved:
            kept, sent = local(functools.partial(halve_kernel, axis, bit), (rows // 2,) * 2, kept, got)
        else:
            (kept,) = local(add_kernel, (rows,), kept, got)
            sent = kept
        got = exchanged(sent, bit, step)
    (value,) = local(add_kernel, kept.shape[:1], kept, got)
    for step, bit in enumerate(reversed(halved), len(bits)):
        got = exchanged(value, bit, step)
        (value,) = local(functools.partial(join_kernel, axis, bit), (2 * value.shape[0],), value, got)
    return value, exchanged(value, bits[0], len(bits) + len(halved))


def body(object_field, probe_modes, measured, row_offset, col_offset, tile_counts):
    axis = "tile"
    slices, _, tile_rows, tile_cols = object_field.shape
    modes, _, width, _ = probe_modes.shape
    slots = measured.shape[0]
    dft, move = complex_tables(width)
    smem = pl.BlockSpec(memory_space=pltpu.SMEM)
    vmem = pl.BlockSpec(memory_space=pltpu.VMEM)
    params = pltpu.CompilerParams(vmem_limit_bytes=16 << 20)

    def held(value):
        return pltpu.with_memory_space_constraint(value, pltpu.VMEM)

    place = jnp.concatenate([row_offset, col_offset])
    before = passed_along(place, axis, 1)

    def load(*arrays):
        return pl.pallas_call(
            load_kernel,
            out_shape=tuple(pltpu.VMEM(a.shape, a.dtype) for a in arrays),
            in_specs=[vmem] * len(arrays),
            out_specs=(vmem,) * len(arrays),
            compiler_params=params,
        )(*arrays)

    (objects,) = load(object_field)
    in_chunk = PAIR

    def windows(size):
        return pltpu.VMEM((size, 2 * slices, width, width), F32)

    rims, strip = [], before
    for start in range(0, slots, in_chunk):
        strip = pl.pallas_call(
            functools.partial(strip_kernel, start),
            out_shape=windows(in_chunk),
            in_specs=[smem, vmem],
            out_specs=vmem,
            compiler_params=params,
        )(after(before, strip), objects)
        rims.append(held(passed_along(strip, axis, -1)))
    tables = [jnp.asarray(t) for t in (*real_forms(dft), *real_forms(move))]
    probe, patterns, *tables = load(*lax.optimization_barrier((strip, probe_modes, measured, *tables))[1:])
    lit = pl.pallas_call(
        functools.partial(light_kernel, axis),
        out_shape=pltpu.VMEM((tile_rows, tile_cols), F32),
        in_specs=[smem, smem, smem, vmem],
        out_specs=vmem,
        compiler_params=params,
    )(tile_counts, place, after(before, strip), probe)
    rows = (2 * modes + 1) * width
    whole, half = pltpu.VMEM((rows, width), F32), pltpu.VMEM((rows // 2, width), F32)
    common = (probe, patterns, *tables)
    grads, arrived, sums = [], [], []
    for start in range(0, slots, PAIR):
        last_call = start + PAIR == slots
        ready = arrived[: start // PAIR - 1] if start else [lit]
        pieces = [windows(size) for _, size in PIECES] if last_call else [windows(PAIR)]
        results = pieces + ([half, half] if last_call else [whole])
        outs = pl.pallas_call(
            functools.partial(gradient_kernel, start, axis),
            out_shape=results,
            in_specs=[smem] * 2 + [vmem] * (7 + PAIR + len(sums)),
            out_specs=[vmem] * len(results),
            scratch_shapes=[whole] if last_call else [],
            compiler_params=params,
            cost_estimate=pl.CostEstimate(flops=1, bytes_accessed=6 << 20, transcendentals=0),
        )(
            tile_counts, after(place, *ready), objects, *common,
            *(rims[(start + i) // in_chunk] for i in range(PAIR)), *sums,
        )
        grads += outs[: len(pieces)]
        sums = outs[len(pieces) :]
        if not last_call:
            arrived.append(passed_along(outs[0], axis, 1))

    def beside(step, value):
        for n, (when, size) in enumerate(PIECES):
            if when == step:
                piece = pl.pallas_call(
                    copy_kernel,
                    out_shape=windows(size),
                    in_specs=[vmem],
                    out_specs=vmem,
                    compiler_params=params,
                    cost_estimate=pl.CostEstimate(flops=1, bytes_accessed=6 << 20, transcendentals=0),
                )(after(grads[n - len(PIECES)], value))
                arrived.append(passed_along(piece, axis, 1))

    updated = []

    def waits(step):
        if step == 3:
            return arrived[: (1 if step == 3 else 9)]
        last = lax.axis_size(axis).bit_length() - 1 + 2
        if step == last - 1:
            return arrived[: (1 if step == 3 else 9)]
        if step == last:
            updated.append(update())
            return updated
        return []

    def update():
        return pl.pallas_call(
            functools.partial(update_kernel, axis),
            grid=(2 * slices,),
            out_shape=jax.ShapeDtypeStruct(object_field.shape, F32),
            in_specs=[smem] * 3 + [vmem] * (2 + 2 * len(grads)),
            out_specs=pl.BlockSpec((1, 1, tile_rows, tile_cols), lambda plane: (plane // 2, plane % 2, 0, 0)),
            scratch_shapes=[pltpu.VMEM((tile_rows, tile_cols), F32)],
            compiler_params=params,
            cost_estimate=pl.CostEstimate(flops=1, bytes_accessed=12 << 20, transcendentals=0),
        )(tile_counts, place, before, objects, lit, *grads, *map(held, arrived))

    mine, got = half_sum(*sums, axis, beside, waits)
    updated_probe = pl.pallas_call(
        functools.partial(probe_kernel, axis),
        out_shape=jax.ShapeDtypeStruct(probe_modes.shape, F32),
        in_specs=[vmem] * 3,
        out_specs=vmem,
        scratch_shapes=[pltpu.VMEM((rows, width), F32)],
        compiler_params=params,
    )(mine, got, probe)
    return (updated[0], updated_probe)


def solution(mesh):
    return jax.shard_map(
        body,
        mesh=mesh,
        in_specs=(
            P("groups", None, "tile", None),
            P("groups", None, None, None),
            P(("groups", "tile"), None, None),
            P(("groups", "tile")),
            P(("groups", "tile")),
            P("groups"),
        ),
        out_specs=(P("groups", None, "tile", None), P("groups", None, None, None)),
        check_vma=False,
    )
```

```python
import functools
import math

import jax
import jax.numpy as jnp
import ml_dtypes
import numpy as np
from jax import lax
from jax.experimental import pallas as pl
from jax.experimental.pallas import tpu as pltpu
from jax.sharding import PartitionSpec as P

F32, BF16 = jnp.float32, jnp.bfloat16


def passed_along(value, axis, steps):
    count = lax.axis_size(axis)
    leading, last = (max(0, -steps), min(count, count - steps))
    return lax.ppermute(value, axis, [(source, source + steps) for source in range(leading, last)])


def complex_tables(width):
    index = np.arange(width)
    angle = 2.0 * math.pi / width * (index[:, None] * index[None, :] % width)
    dft = np.exp(-1j * angle) / math.sqrt(width)
    frequency = np.where(index < width // 2, index, index - width).astype(np.float64)
    phase = np.exp(-0.5j * math.pi / width * frequency**2)
    return dft, np.conj(dft) @ (phase[:, None] * dft)


def real_forms(table):
    re, im = table.real, table.imag
    right = np.block([[re, im], [-im, re]])
    left = np.block([[re, -im], [im, re]])

    def parts(matrix):
        high = matrix.astype(ml_dtypes.bfloat16)
        low = (matrix - high.astype(np.float64)).astype(ml_dtypes.bfloat16)
        return high, low

    right_high, right_low = parts(right)
    left_high, left_low = parts(left)
    return np.stack([right_high, right_low]), np.concatenate([left_high, left_low], 0)


def halves(value):
    high = value.astype(BF16)
    return high, (value - high.astype(F32)).astype(BF16)


def dot(left, right):
    return jnp.dot(left, right, preferred_element_type=F32)


def right_stage(blocks, right_ref):
    rows = jnp.concatenate([jnp.concatenate(pair, 1) for pair in blocks], 0)
    high, low = halves(rows)
    table = jnp.concatenate([right_ref[0], right_ref[0], right_ref[1]], 0)
    return dot(jnp.concatenate([high, low, high], 1), table)


def left_stage(first, width, left_ref):
    modes = first.shape[0] // width
    cols = jnp.concatenate(
        [
            jnp.concatenate(
                [first[m * width : (m + 1) * width, part * width : (part + 1) * width] for m in range(modes)], 1
            )
            for part in range(2)
        ],
        0,
    )
    high, low = halves(cols)
    table = jnp.concatenate([left_ref[: 2 * width], left_ref[: 2 * width], left_ref[2 * width :]], 1)
    second = dot(table, jnp.concatenate([high, low, high], 0))
    return [
        (second[:width, m * width : (m + 1) * width], second[width:, m * width : (m + 1) * width])
        for m in range(modes)
    ]


def two_sided(blocks, right_ref, left_ref, group=4):
    width = blocks[0][0].shape[0]
    firsts = [right_stage(blocks[i : i + group], right_ref) for i in range(0, len(blocks), group)]
    return [block for first in firsts for block in left_stage(first, width, left_ref)]


def times(left, right):
    return left[0] * right[0] - left[1] * right[1], left[0] * right[1] + left[1] * right[0]


def window_place(place_ref, slot, slots, width, blocks):
    row_start, col_start = place_ref[slot], place_ref[slots + slot]
    block = col_start // width
    shift = col_start - block * width
    lane = lax.broadcasted_iota(jnp.int32, (width, width), 1)
    row = lax.broadcasted_iota(jnp.int32, (width, width), 0)
    first = pl.ds(pl.multiple_of(block * width, width), width)
    second = pl.ds(pl.multiple_of(jnp.minimum(block + 1, blocks - 1) * width, width), width)
    return row >= row_start, lane >= shift, shift, first, second


def load_kernel(*refs):
    count = len(refs) // 2
    for source, target in zip(refs[:count], refs[count:]):
        target[...] = source[...]


def strip_kernel(start, before_ref, object_ref, strip_ref):
    size, planes, width, _ = strip_ref.shape
    slots = before_ref.shape[0] // 2
    for i in range(size):
        _, in_first, _, first, second = window_place(before_ref, start + i, slots, width, object_ref.shape[-1] // width)
        for plane in range(planes):
            strip_ref[i, plane] = jnp.where(
                in_first, object_ref[plane // 2, plane % 2, :, first], object_ref[plane // 2, plane % 2, :, second]
            )


PAIR = 3
PIECES = ((0, 1), (1, 1), (2, 1))


def gradient_kernel(
    start, axis, counts_ref, place_ref, object_ref, probe_ref, measured_ref, fr_ref, fl_ref, pr_ref, pl_ref, *refs
):
    first_call = start == 0
    tile = lax.axis_index(axis)
    count = counts_ref[tile]
    modes, _, width, _ = probe_ref.shape
    slots = measured_ref.shape[0]
    last_call = start + PAIR == slots
    rim_refs, refs = refs[:PAIR], refs[PAIR:]
    before, refs = (refs[:1], refs[1:]) if not first_call else ((), refs)
    if last_call:
        *grad_refs, kept_ref, sent_ref, sums_ref = refs
    else:
        *grad_refs, sums_ref = refs
    sums_ref[...] = jnp.zeros(sums_ref.shape, F32) if first_call else before[0][...]
    probe = [(probe_ref[m, 0], probe_ref[m, 1]) for m in range(modes)]

    @pl.when(start < count)
    def _():
        places = [
            window_place(place_ref, start + i, slots, width, object_ref.shape[-1] // width) for i in range(PAIR)
        ]

        def window(i, s, part):
            in_own, in_first, shift, first, second = places[i]
            own = jnp.where(in_first, object_ref[s, part, :, first], object_ref[s, part, :, second])
            rim_ref = rim_refs[i]
            stored = jnp.where(in_own, own, rim_ref[(start + i) % rim_ref.shape[0], 2 * s + part])
            stored = pltpu.roll(stored, lax.rem(width - place_ref[start + i], width), 0)
            return pltpu.roll(stored, lax.rem(width - shift, width), 1)

        def put(i, s, part, value):
            value = pltpu.roll(value, place_ref[start + i], 0)
            grad_ref, at = [(ref, at) for ref in grad_refs for at in range(ref.shape[0])][i]
            grad_ref[at, 2 * s + part] = pltpu.roll(value, places[i][2], 1)

        def split(blocks):
            return [blocks[i * modes : (i + 1) * modes] for i in range(PAIR)]

        ones = [(window(i, 0, 0), window(i, 0, 1)) for i in range(PAIR)]
        moved = split(two_sided([times(p, one) for one in ones for p in probe], pr_ref, pl_ref))
        twos = [(window(i, 1, 0), window(i, 1, 1)) for i in range(PAIR)]
        far = split(two_sided([times(w, two) for ws, two in zip(moved, twos) for w in ws], fr_ref, fl_ref))
        back = []
        for i in range(PAIR):
            intensity = sum(re * re + im * im for re, im in far[i])
            residue = 2.0 * (intensity - measured_ref[start + i])
            back += [(residue * re, -(residue * im)) for re, im in far[i]]
        back = split(two_sided(back, fr_ref, fl_ref))
        last = split(two_sided([times(g, two) for gs, two in zip(back, twos) for g in gs], pr_ref, pl_ref))
        for i in range(PAIR):
            terms = [times(w, g) for w, g in zip(moved[i], back[i])]
            put(i, 1, 0, sum(t[0] for t in terms))
            put(i, 1, 1, -sum(t[1] for t in terms))
            terms = [times(p, g) for p, g in zip(probe, last[i])]
            put(i, 0, 0, sum(t[0] for t in terms))
            put(i, 0, 1, -sum(t[1] for t in terms))
        live = [start + i < count for i in range(PAIR)]

        def summed(values):
            return sum(jnp.where(alive, value, 0.0) for alive, value in zip(live, values))

        for m in range(modes):
            grads = [times(one, g[m]) for one, g in zip(ones, last)]
            for part, sign in ((0, 1.0), (1, -1.0)):
                rows = pl.ds((2 * m + part) * width, width)
                sums_ref[rows] += sign * summed(g[part] for g in grads)
        sums_ref[pl.ds(2 * modes * width, width)] += summed(re * re + im * im for re, im in ones)
    if last_call:
        half = kept_ref.shape[0]
        side = lax.rem(tile, 2)
        kept_ref[...] = sums_ref[pl.ds(pl.multiple_of(side * half, 8), half)]
        sent_ref[...] = sums_ref[pl.ds(pl.multiple_of((1 - side) * half, 8), half)]


def add_windows(target_ref, counts_ref, place_ref, before_ref, axis, window_of):
    tile = lax.axis_index(axis)
    width, slots = target_ref.shape[0], place_ref.shape[0] // 2
    target_ref[...] = jnp.zeros(target_ref.shape, F32)
    for slot in range(slots):
        for own in (True, False):
            ref = place_ref if own else before_ref
            count = counts_ref[tile] if own else jnp.where(tile > 0, counts_ref[jnp.maximum(tile - 1, 0)], 0)

            @pl.when(slot < count)
            def _():
                in_own, in_first, shift, first, second = window_place(
                    ref, slot, slots, width, target_ref.shape[1] // width
                )
                value = window_of(ref, slot, own, shift)
                wanted = in_own if own else jnp.logical_not(in_own)
                value = jnp.where(wanted, value, 0.0)
                target_ref[:, first] += jnp.where(in_first, value, 0.0)
                target_ref[:, second] += jnp.where(in_first, 0.0, value)


def light_kernel(axis, counts_ref, place_ref, before_ref, probe_ref, lit_ref):
    modes = probe_ref.shape[0]
    power = sum(probe_ref[m, part] * probe_ref[m, part] for m in range(modes) for part in range(2))

    def window_of(ref, slot, own, shift):
        return pltpu.roll(pltpu.roll(power, ref[slot], 0), shift, 1)

    add_windows(lit_ref, counts_ref, place_ref, before_ref, axis, window_of)
    lit_ref[...] = 0.5 / (lit_ref[...] + 1.0)


def copy_kernel(source_ref, out_ref):
    out_ref[...] = source_ref[...]


def update_kernel(axis, counts_ref, place_ref, before_ref, object_ref, lit_ref, *refs):
    *refs, out_ref, sum_ref = refs
    plane = pl.program_id(0)
    own_refs, rim_refs = refs[: len(refs) // 2], refs[len(refs) // 2 :]

    def window_of(ref, slot, own, shift):
        parts = [(r, i) for r in (own_refs if own else rim_refs) for i in range(r.shape[0])]
        return parts[slot][0][parts[slot][1], plane]

    add_windows(sum_ref, counts_ref, place_ref, before_ref, axis, window_of)
    out_ref[0, 0] = object_ref[plane // 2, plane % 2] - sum_ref[...] * lit_ref[...]


def probe_kernel(axis, mine_ref, got_ref, probe_ref, out_ref, total_ref):
    modes, _, width, _ = probe_ref.shape
    half = mine_ref.shape[0]
    side = lax.rem(lax.axis_index(axis), 2)
    total_ref[pl.ds(pl.multiple_of(side * half, 8), half)] = mine_ref[...]
    total_ref[pl.ds(pl.multiple_of((1 - side) * half, 8), half)] = got_ref[...]
    scale = 0.5 / (total_ref[pl.ds(2 * modes * width, width)] + 1.0)
    for m in range(modes):
        for part in range(2):
            out_ref[m, part] = probe_ref[m, part] - total_ref[pl.ds((2 * m + part) * width, width)] * scale


def after(value, *others):
    return lax.optimization_barrier((value, *others))[0]


def halve_kernel(axis, bit, kept_ref, got_ref, next_kept_ref, next_sent_ref):
    half = next_kept_ref.shape[0]
    side = lax.rem(lax.axis_index(axis) // bit, 2)
    for ref, which in ((next_kept_ref, side), (next_sent_ref, 1 - side)):
        rows = pl.ds(pl.multiple_of(which * half, 8), half)
        ref[...] = kept_ref[rows] + got_ref[rows]


def add_kernel(kept_ref, got_ref, out_ref):
    out_ref[...] = kept_ref[...] + got_ref[...]


def join_kernel(axis, bit, mine_ref, got_ref, out_ref):
    half = mine_ref.shape[0]
    side = lax.rem(lax.axis_index(axis) // bit, 2)
    out_ref[pl.ds(pl.multiple_of(side * half, 8), half)] = mine_ref[...]
    out_ref[pl.ds(pl.multiple_of((1 - side) * half, 8), half)] = got_ref[...]


def half_sum(kept, sent, axis, beside, waits):
    count = lax.axis_size(axis)
    bits = [1 << b for b in range(count.bit_length() - 1)]
    bits = bits[:1] + bits[2:] + bits[1:2]
    vmem = pl.BlockSpec(memory_space=pltpu.VMEM)
    width = kept.shape[1]

    def exchanged(value, bit, step):
        value = after(value, *waits(step))
        got = lax.ppermute(value, axis, [(i, i ^ bit) for i in range(count)])
        beside(step, value)
        return pltpu.with_memory_space_constraint(got, pltpu.VMEM)

    def local(kernel, rows, *operands):
        return pl.pallas_call(
            kernel,
            out_shape=[pltpu.VMEM((n, width), F32) for n in rows],
            in_specs=[vmem] * 2,
            out_specs=[vmem] * len(rows),
            compiler_params=pltpu.CompilerParams(vmem_limit_bytes=4 << 20),
        )(*operands)

    got = exchanged(sent, bits[0], 0)
    halved = bits[1:3]
    for step, bit in enumerate(bits[1:], 1):
        rows = kept.shape[0]
        if bit in halved:
            kept, sent = local(functools.partial(halve_kernel, axis, bit), (rows // 2,) * 2, kept, got)
        else:
            (kept,) = local(add_kernel, (rows,), kept, got)
            sent = kept
        got = exchanged(sent, bit, step)
    (value,) = local(add_kernel, kept.shape[:1], kept, got)
    for step, bit in enumerate(reversed(halved), len(bits)):
        got = exchanged(value, bit, step)
        (value,) = local(functools.partial(join_kernel, axis, bit), (2 * value.shape[0],), value, got)
    return value, exchanged(value, bits[0], len(bits) + len(halved))


def body(object_field, probe_modes, measured, row_offset, col_offset, tile_counts):
    axis = "tile"
    slices, _, tile_rows, tile_cols = object_field.shape
    modes, _, width, _ = probe_modes.shape
    slots = measured.shape[0]
    dft, move = complex_tables(width)
    smem = pl.BlockSpec(memory_space=pltpu.SMEM)
    vmem = pl.BlockSpec(memory_space=pltpu.VMEM)
    params = pltpu.CompilerParams(vmem_limit_bytes=16 << 20)

    def held(value):
        return pltpu.with_memory_space_constraint(value, pltpu.VMEM)

    place = jnp.concatenate([row_offset, col_offset])
    before = passed_along(place, axis, 1)

    def load(*arrays):
        return pl.pallas_call(
            load_kernel,
            out_shape=tuple(pltpu.VMEM(a.shape, a.dtype) for a in arrays),
            in_specs=[vmem] * len(arrays),
            out_specs=(vmem,) * len(arrays),
            compiler_params=params,
        )(*arrays)

    (objects,) = load(object_field)
    in_chunk = PAIR

    def windows(size):
        return pltpu.VMEM((size, 2 * slices, width, width), F32)

    rims, strip = [], before
    for start in range(0, slots, in_chunk):
        strip = pl.pallas_call(
            functools.partial(strip_kernel, start),
            out_shape=windows(in_chunk),
            in_specs=[smem, vmem],
            out_specs=vmem,
            compiler_params=params,
        )(after(before, strip), objects)
        rims.append(held(passed_along(strip, axis, -1)))
    tables = [jnp.asarray(t) for t in (*real_forms(dft), *real_forms(move))]
    probe, patterns, *tables = load(*lax.optimization_barrier((strip, probe_modes, measured, *tables))[1:])
    lit = pl.pallas_call(
        functools.partial(light_kernel, axis),
        out_shape=pltpu.VMEM((tile_rows, tile_cols), F32),
        in_specs=[smem, smem, smem, vmem],
        out_specs=vmem,
        compiler_params=params,
    )(tile_counts, place, after(before, strip), probe)
    rows = (2 * modes + 1) * width
    whole, half = pltpu.VMEM((rows, width), F32), pltpu.VMEM((rows // 2, width), F32)
    common = (probe, patterns, *tables)
    grads, arrived, sums = [], [], []
    for start in range(0, slots, PAIR):
        last_call = start + PAIR == slots
        ready = arrived[: start // PAIR - 1] if start else [lit]
        pieces = [windows(size) for _, size in PIECES] if last_call else [windows(PAIR)]
        results = pieces + ([half, half] if last_call else [whole])
        outs = pl.pallas_call(
            functools.partial(gradient_kernel, start, axis),
            out_shape=results,
            in_specs=[smem] * 2 + [vmem] * (7 + PAIR + len(sums)),
            out_specs=[vmem] * len(results),
            scratch_shapes=[whole] if last_call else [],
            compiler_params=params,
            cost_estimate=pl.CostEstimate(flops=1, bytes_accessed=6 << 20, transcendentals=0),
        )(
            tile_counts, after(place, *ready), objects, *common,
            *(rims[(start + i) // in_chunk] for i in range(PAIR)), *sums,
        )
        grads += outs[: len(pieces)]
        sums = outs[len(pieces) :]
        if not last_call:
            arrived.append(passed_along(outs[0], axis, 1))

    def beside(step, value):
        for n, (when, size) in enumerate(PIECES):
            if when == step:
                piece = pl.pallas_call(
                    copy_kernel,
                    out_shape=windows(size),
                    in_specs=[vmem],
                    out_specs=vmem,
                    compiler_params=params,
                    cost_estimate=pl.CostEstimate(flops=1, bytes_accessed=6 << 20, transcendentals=0),
                )(after(grads[n - len(PIECES)], value))
                arrived.append(passed_along(piece, axis, 1))

    updated = []

    def waits(step):
        if step == 3:
            return arrived[: (1 if step == 3 else 9)]
        last = lax.axis_size(axis).bit_length() - 1 + 2
        if step == last - 1:
            return arrived[: (1 if step == 3 else 9)]
        if step == last:
            updated.append(update())
            return updated
        return []

    def update():
        return pl.pallas_call(
            functools.partial(update_kernel, axis),
            grid=(2 * slices,),
            out_shape=jax.ShapeDtypeStruct(object_field.shape, F32),
            in_specs=[smem] * 3 + [vmem] * (2 + 2 * len(grads)),
            out_specs=pl.BlockSpec((1, 1, tile_rows, tile_cols), lambda plane: (plane // 2, plane % 2, 0, 0)),
            scratch_shapes=[pltpu.VMEM((tile_rows, tile_cols), F32)],
            compiler_params=params,
            cost_estimate=pl.CostEstimate(flops=1, bytes_accessed=12 << 20, transcendentals=0),
        )(tile_counts, place, before, objects, lit, *grads, *map(held, arrived))

    mine, got = half_sum(*sums, axis, beside, waits)
    updated_probe = pl.pallas_call(
        functools.partial(probe_kernel, axis),
        out_shape=jax.ShapeDtypeStruct(probe_modes.shape, F32),
        in_specs=[vmem] * 3,
        out_specs=vmem,
        scratch_shapes=[pltpu.VMEM((rows, width), F32)],
        compiler_params=params,
    )(mine, got, probe)
    return (updated[0], updated_probe)


def solution(mesh):
    return jax.shard_map(
        body,
        mesh=mesh,
        in_specs=(
            P("groups", None, "tile", None),
            P("groups", None, None, None),
            P(("groups", "tile"), None, None),
            P(("groups", "tile")),
            P(("groups", "tile")),
            P("groups"),
        ),
        out_specs=(P("groups", None, "tile", None), P("groups", None, None, None)),
        check_vma=False,
    )
```
